32 devices in a mesh: seq: 2 (over y), fsdp: 16 (over z, x, core).
Axes of the slice: x: 2, y: 2, z: 4, core: 2. Of those that a mesh axis runs over, the one named last changes fastest.
Arguments:
- tokens: bfloat16 [16, 1024, 2048], P('fsdp', 'seq'), may hold values from -6 to 6
- segments: int32 [16, 1024], P('fsdp'), may hold values from -1 to 16, as said below
- attn_gain: bfloat16 [2048], P(('seq', 'fsdp')), may hold values from 0.5 to 1.5
- w_query: bfloat16 [2048, 1536], P(('seq', 'fsdp')), may hold values from -0.125 to 0.125
- key_projection_weight: bfloat16 [2048, 384], P(('seq', 'fsdp')), may hold values from -0.125 to 0.125
- value_projection_weight: bfloat16 [2048, 384], P(('seq', 'fsdp')), may hold values from -0.125 to 0.125
- query_norm_gain: bfloat16 [64], replicated, may hold values from 0.099609375 to 1.8984375
- key_gain: bfloat16 [64], replicated, may hold values from 0.099609375 to 1.8984375
- w_out: bfloat16 [1536, 2048], P(('seq', 'fsdp')), may hold values from -0.625 to 0.625
- ffn_gain: bfloat16 [2048], P(('seq', 'fsdp')), may hold values from 0.5 to 1.5
- w_gate: bfloat16 [2048, 4864], P(('seq', 'fsdp')), may hold values from -0.125 to 0.125
- w_up: bfloat16 [2048, 4864], P(('seq', 'fsdp')), may hold values from -0.125 to 0.125
- w_down: bfloat16 [4864, 2048], P(('seq', 'fsdp')), may hold values from -0.078125 to 0.078125
- cotangent: bfloat16 [16, 1024, 2048], P('fsdp', 'seq'), may hold values from -6 to 6
Outputs:
- output: bfloat16 [16, 1024, 2048], P('fsdp', 'seq')
- input_grad: float32 [16, 1024, 2048], P('fsdp', 'seq')
- attn_gain_grad: float32 [2048], P(('seq', 'fsdp'))
- w_query_grad: float32 [2048, 1536], P(('seq', 'fsdp'))
- w_key_grad: float32 [2048, 384], P(('seq', 'fsdp'))
- w_value_grad: float32 [2048, 384], P(('seq', 'fsdp'))
- query_gain_grad: float32 [64], replicated
- key_gain_grad: float32 [64], replicated
- w_out_grad: float32 [1536, 2048], P(('seq', 'fsdp'))
- ffn_gain_grad: float32 [2048], P(('seq', 'fsdp'))
- w_gate_grad: float32 [2048, 4864], P(('seq', 'fsdp'))
- w_up_grad: float32 [2048, 4864], P(('seq', 'fsdp'))
- w_down_grad: float32 [4864, 2048], P(('seq', 'fsdp'))
The draws below stay inside these ranges and needn't reach their ends.
Inputs may be any that keep to these rules, and one draw needn't show every extreme that they name: `segments`: in each sequence ids start at 0, rise by one at each new document and end at min(16, 128) before a tail of -1 that fills 1 to 128 positions; in each sequence one document covers the positions 511 and 512.
All inputs are finite; a program needn't handle non-finite values.
Results may differ from the reference program's by a relative error of at most 0.015.
Values may be sent and summed in bfloat16 or wider, within the bound.
No kernel may reach another device: no remote copies, remote signals or barrier semaphores. Data moves between devices by JAX's collectives and lax.ppermute only.
A program may use at most 384 MiB of HBM per device.

```python
import math
import jax
import jax.numpy as jnp
from jax import lax

MODEL_WIDTH = 2048
QUERY_HEADS = 24
KEY_VALUE_HEADS = 6
HEAD_SIZE = 64
FF = 4864
LEN = 1024
HALF = 512
NSEQ = 16


def draw_segments(key, part):
    places = jnp.arange(LEN, dtype=jnp.int32)
    cut_total = min(16, LEN // 8)

    def draw_row(row_key):
        key_score, key_before, key_after, key_pad = jax.random.split(row_key, 4)
        before = jax.random.randint(key_before, (), HALF // 8, HALF // 2 + 1)
        after = jax.random.randint(key_after, (), HALF // 8, HALF // 2 + 1)
        pad_len = jax.random.randint(key_pad, (), 1, LEN // 8 + 1)
        outside = (places <= HALF - before) | (places > HALF + after)
        usable = outside & (places >= 1) & (places < LEN - pad_len)
        raw_score = jax.random.randint(key_score, (LEN,), 0, LEN)
        score = raw_score * (LEN - places) * LEN + places
        score = jnp.where(usable, score, -1 - places)
        picked = lax.top_k(score, cut_total)[1]
        is_cut = jnp.any(picked[:, None] == places[None, :], axis=0)
        seg_ids = jnp.cumsum(is_cut.astype(jnp.int32))
        return jnp.where(places >= LEN - pad_len, -1, seg_ids).astype(jnp.int32)
    row_keys = jax.random.split(key, NSEQ)
    return jax.vmap(draw_row)(row_keys)


def shard_levels(own_key, extent, pieces, low, largest):
    factor_of = 1.0
    for position, shards_of in pieces:
        heights = jax.random.uniform(jax.random.fold_in(jax.random.fold_in(own_key, 6), position), (shards_of,), jnp.float32, low / len(pieces), largest / len(pieces))
        factor_of = factor_of * jnp.repeat(jnp.exp(heights), extent[position] // shards_of).reshape((-1,) + (1,) * (len(extent) - 1 - position))
    return factor_of


def scatter_about(rng, shape, spread, limit, pieces=(), kind=jnp.bfloat16):
    entries = spread * jax.random.normal(rng, shape, jnp.float32)
    if pieces:
        entries = entries * shard_levels(rng, shape, pieces, -0.22, 0.18)
    return jnp.clip(entries, -limit, limit).astype(kind)


def setup_inputs(seed: int = 0) -> dict:
    arg_keys = jax.random.split(jax.random.key(seed), 15)
    tokens = scatter_about(arg_keys[0], (NSEQ, LEN, MODEL_WIDTH), 1.0, 6.0, ((0, 16), (1, 2)))
    segments = draw_segments(jax.random.fold_in(arg_keys[14], 71), 0)
    attn_gain = jnp.clip(1.0 + 0.1 * jax.random.normal(arg_keys[2], (MODEL_WIDTH,), jnp.float32), 0.5, 1.5).astype(jnp.bfloat16)
    w_query = scatter_about(arg_keys[3], (MODEL_WIDTH, QUERY_HEADS * HEAD_SIZE), MODEL_WIDTH ** -0.5, 0.125, ((0, 32),))
    key_projection_weight = scatter_about(arg_keys[4], (MODEL_WIDTH, KEY_VALUE_HEADS * HEAD_SIZE), MODEL_WIDTH ** -0.5, 0.125, ((0, 32),))
    value_projection_weight = scatter_about(arg_keys[5], (MODEL_WIDTH, KEY_VALUE_HEADS * HEAD_SIZE), MODEL_WIDTH ** -0.5, 0.125, ((0, 32),))
    query_norm_gain = jnp.clip(1.0 + 0.18 * jax.random.normal(arg_keys[6], (HEAD_SIZE,), jnp.float32), 0.099609375, 1.8984375).astype(jnp.bfloat16)
    key_gain = jnp.clip(1.0 + 0.18 * jax.random.normal(arg_keys[7], (HEAD_SIZE,), jnp.float32), 0.099609375, 1.8984375).astype(jnp.bfloat16)
    w_out = scatter_about(arg_keys[8], (QUERY_HEADS * HEAD_SIZE, MODEL_WIDTH), (QUERY_HEADS * HEAD_SIZE // 16) ** -0.5, 0.625, ((0, 32),))
    ffn_gain = jnp.clip(1.0 + 0.1 * jax.random.normal(arg_keys[9], (MODEL_WIDTH,), jnp.float32), 0.5, 1.5).astype(jnp.bfloat16)
    w_gate = scatter_about(arg_keys[10], (MODEL_WIDTH, FF), MODEL_WIDTH ** -0.5, 0.125, ((0, 32),))
    w_up = scatter_about(arg_keys[11], (MODEL_WIDTH, FF), MODEL_WIDTH ** -0.5, 0.125, ((0, 32),))
    w_down = scatter_about(arg_keys[12], (FF, MODEL_WIDTH), FF ** -0.5, 0.078125, ((0, 32),))
    cotangent = scatter_about(arg_keys[13], (NSEQ, LEN, MODEL_WIDTH), 1.0, 6.0, ((0, 16), (1, 2)))
    return dict(tokens=tokens, segments=segments, attn_gain=attn_gain, w_query=w_query, key_projection_weight=key_projection_weight, value_projection_weight=value_projection_weight, query_norm_gain=query_norm_gain, key_gain=key_gain, w_out=w_out, ffn_gain=ffn_gain, w_gate=w_gate, w_up=w_up, w_down=w_down, cotangent=cotangent)


@jax.custom_vjp
def narrow_cast(v):
    return lax.optimization_barrier(v.astype(jnp.bfloat16)).astype(jnp.float32)

@jax.custom_vjp
def narrow_backward(v):
    return v

def low_keep(v):
    return (narrow_cast(v), None)

def low_pass(kept, grad):
    return (grad,)

def back_keep(v):
    return (v, None)

def back_low(kept, grad):
    return (narrow_cast(grad),)
narrow_cast.defvjp(low_keep, low_pass)
narrow_backward.defvjp(back_keep, back_low)
EPS = 1e-06

def row_norm_apply(values, gain_vec):
    return values * lax.rsqrt(lax.optimization_barrier(jnp.mean(values * values, axis=-1, keepdims=True)) + EPS) * gain_vec

def apply_rotary(tensor, cosine_table, sine_table):
    middle = tensor.shape[-1] // 2
    former = tensor[..., :middle]
    latter = tensor[..., middle:]
    return jnp.concatenate([former * cosine_table - latter * sine_table, latter * cosine_table + former * sine_table], axis=-1)

def doc_positions(segment_row):
    packed_length = segment_row.shape[-1]
    places = jnp.arange(packed_length, dtype=jnp.int32)
    earlier = jnp.concatenate([segment_row[..., :1] + 1, segment_row[..., :-1]], axis=-1)
    starts = jnp.where(segment_row != earlier, places, 0).astype(jnp.int32)
    return places - lax.cummax(starts, axis=segment_row.ndim - 1)

def rotary_tables(positions):
    pair_count = HEAD_SIZE // 2
    frequencies = jnp.exp(jnp.arange(pair_count, dtype=jnp.float32) * (-2.0 * math.log(10000.0) / HEAD_SIZE))
    phases = positions.astype(jnp.float32)[..., None] * frequencies
    return (jnp.cos(phases)[..., None, :], jnp.sin(phases)[..., None, :])

def block_forward(parameters, inputs, segment_row):
    attn_gain, w_query, key_projection_weight, value_projection_weight, query_norm_gain, key_gain, w_out, ffn_gain, w_gate, w_up, w_down = parameters
    highest_precision = lax.Precision.HIGHEST
    packed_length = inputs.shape[0]
    head_groups = QUERY_HEADS // KEY_VALUE_HEADS
    score_scale = HEAD_SIZE ** (-0.5)
    first_hidden = narrow_cast(row_norm_apply(inputs, attn_gain))
    query_rows = narrow_backward(jnp.dot(first_hidden, w_query, precision=highest_precision)).reshape(packed_length, QUERY_HEADS, HEAD_SIZE)
    key_unnormed = narrow_backward(jnp.dot(first_hidden, key_projection_weight, precision=highest_precision)).reshape(packed_length, KEY_VALUE_HEADS, HEAD_SIZE)
    value_narrow = narrow_cast(narrow_backward(jnp.dot(first_hidden, value_projection_weight, precision=highest_precision))).reshape(packed_length, KEY_VALUE_HEADS, HEAD_SIZE)
    cosine_table, sine_table = rotary_tables(doc_positions(segment_row))
    query_rotary = narrow_cast(apply_rotary(row_norm_apply(query_rows, query_norm_gain), cosine_table, sine_table)).reshape(packed_length, KEY_VALUE_HEADS, head_groups, HEAD_SIZE)
    key_rotary = narrow_cast(apply_rotary(row_norm_apply(key_unnormed, key_gain), cosine_table, sine_table))
    places = jnp.arange(packed_length, dtype=jnp.int32)
    allowed = (segment_row[:, None] == segment_row[None, :]) & (places[None, :] <= places[:, None])
    scores = narrow_backward(jnp.einsum('qhgd,khd->hgqk', query_rotary, key_rotary, precision=highest_precision) * score_scale)
    scores = jnp.where(allowed, scores, -1e+30)
    row_peak = lax.optimization_barrier(jnp.max(scores, axis=-1, keepdims=True))
    expo_terms = jnp.exp(scores - row_peak)
    probs = narrow_cast(expo_terms / lax.optimization_barrier(jnp.sum(expo_terms, axis=-1, keepdims=True)))
    attn = jnp.einsum('hgqk,khd->qhgd', probs, value_narrow, precision=highest_precision).reshape(packed_length, QUERY_HEADS * HEAD_SIZE)
    attn = narrow_cast(narrow_backward(attn))
    middle = inputs + narrow_backward(jnp.dot(attn, w_out, precision=highest_precision))
    hidden_second = narrow_cast(row_norm_apply(middle, ffn_gain))
    gate_pre = narrow_backward(jnp.dot(hidden_second, w_gate, precision=highest_precision))
    up_pre = narrow_backward(jnp.dot(hidden_second, w_up, precision=highest_precision))
    act_low = narrow_cast(jax.nn.silu(gate_pre) * up_pre)
    return middle + narrow_backward(jnp.dot(act_low, w_down, precision=highest_precision))

def reference(tokens, segments, attn_gain, w_query, key_projection_weight, value_projection_weight, query_norm_gain, key_gain, w_out, ffn_gain, w_gate, w_up, w_down, cotangent):
    parameters = tuple((entry.astype(jnp.float32) for entry in (attn_gain, w_query, key_projection_weight, value_projection_weight, query_norm_gain, key_gain, w_out, ffn_gain, w_gate, w_up, w_down)))

    def scan_step(totals, bundle):
        seq_tokens, segment_row, seq_grad = bundle

        def forward_fn(params_in, inputs):
            return block_forward(params_in, inputs, segment_row)
        block_out, pullback = jax.vjp(forward_fn, parameters, seq_tokens.astype(jnp.float32))
        grad_params, grad_tokens = pullback(seq_grad.astype(jnp.float32))
        new_totals = tuple((left_sum + right_sum for left_sum, right_sum in zip(totals, grad_params)))
        return (new_totals, (block_out.astype(jnp.bfloat16), grad_tokens))
    zero_grads = tuple((jnp.zeros(entry.shape, jnp.float32) for entry in parameters))
    totals, (outputs, input_grad) = lax.scan(scan_step, zero_grads, (tokens, segments, cotangent))
    return (outputs, input_grad, totals[0], totals[1], totals[2], totals[3], totals[4], totals[5], totals[6], totals[7], totals[8], totals[9], totals[10])
```

```python
import functools
import math

import jax
import jax.numpy as jnp
from jax import lax
from jax.experimental import pallas as pl
from jax.experimental.pallas import tpu as pltpu
from jax.sharding import Mesh, PartitionSpec as P

EPS = 1e-06
BF = jnp.bfloat16
F32 = jnp.float32
HEAD_SIZE = 64
TILE = 128
SCALE = HEAD_SIZE ** (-0.5)
VMEM_LIMIT = 56 * 2**20


def dot(a, b):
    return lax.dot_general(a, b, (((1,), (0,)), ((), ())), preferred_element_type=F32)


def dot_nt(a, b):
    return lax.dot_general(a, b, (((1,), (1,)), ((), ())), preferred_element_type=F32)


def dot_tn(a, b):
    return lax.dot_general(a, b, (((0,), (0,)), ((), ())), preferred_element_type=F32)


def call(kernel, grid, in_specs, out_specs, out_shape, name, scratch=(), scalars=()):
    scalars = [jnp.asarray(s, jnp.int32).reshape(-1) for s in scalars]
    return functools.partial(
        pl.pallas_call(
            kernel,
            grid_spec=pltpu.PrefetchScalarGridSpec(
                num_scalar_prefetch=len(scalars),
                grid=grid,
                in_specs=in_specs,
                out_specs=out_specs,
                scratch_shapes=scratch,
            ),
            out_shape=out_shape,
            compiler_params=pltpu.CompilerParams(vmem_limit_bytes=VMEM_LIMIT),
            name=name,
        ),
        *scalars,
    )


def shaped(shape, dtype):
    return jax.ShapeDtypeStruct(shape, dtype)


def whole(shape):
    return pl.BlockSpec(shape, lambda *_: (0,) * len(shape))


def once(shape):
    return pl.BlockSpec(shape, lambda *_: (0,) * len(shape), pipeline_mode=pl.Buffered(1))


def row_blocks(tile, cols):
    return pl.BlockSpec((tile, cols), lambda i, *_: (i, 0))


def group_blocks(tile, cols, group, per_group):
    return pl.BlockSpec(
        (tile, cols), lambda i, *_: (jnp.clip(i - group * per_group, 0, per_group - 1), 0)
    )


def pick_group(refs, per_group):
    value = refs[0][...]
    for g in range(1, len(refs)):
        value = jnp.where(pl.program_id(0) >= g * per_group, refs[g][...], value)
    return value


def lane_of(shape):
    return lax.broadcasted_iota(jnp.int32, shape, 1)


def half_sums(values, even):
    low = jnp.sum(jnp.where(even, values, 0.0), axis=-1, keepdims=True)
    high = jnp.sum(jnp.where(even, 0.0, values), axis=-1, keepdims=True)
    return jnp.where(even, low, high)


def turned(values, first):
    return jnp.where(first, pltpu.roll(values, TILE - 32, 1), pltpu.roll(values, 32, 1))


def project(groups, weight_all, core, q_gain, k_gain, cos, sin, q_cols, kv_cols):
    half, width = groups[0].shape
    cols = q_cols + 2 * kv_cols
    q_tiles, k_heads = q_cols // TILE, kv_cols // HEAD_SIZE
    raw_cols = (q_tiles + (k_heads + 1) // 2) * TILE
    tile = 256
    per = half // tile
    count = len(groups)
    rows = count * half

    def kernel(core_ref, *refs):
        hid, (w_ref, qg_ref, kg_ref, cos_ref, sin_ref, q_ref, kv_ref, raw_ref) = refs[:count], refs[count:]
        lane = lane_of((tile, TILE))
        even, first = lane < HEAD_SIZE, lane % HEAD_SIZE < HEAD_SIZE // 2
        out = dot(pick_group(hid, per), w_ref[...])
        cos, sin = cos_ref[...], sin_ref[...]
        raw_ref[...] = out[:, :raw_cols]
        for t in range(cols // TILE):
            x = out[:, t * TILE : (t + 1) * TILE]
            heads_left = k_heads - 2 * (t - q_tiles)
            y = x
            if heads_left > 0:
                gain = qg_ref[...] if t < q_tiles else kg_ref[...]
                y = x * lax.rsqrt(half_sums(x * x, even) * (1.0 / HEAD_SIZE) + EPS) * gain
                y = y * cos + turned(y, first) * sin
                if t >= q_tiles and heads_left == 1:
                    y = jnp.where(even, y, x)
            if t < q_tiles:
                q_ref[:, t * TILE : (t + 1) * TILE] = y.astype(BF)
            else:
                kv_ref[:, (t - q_tiles) * TILE : (t - q_tiles + 1) * TILE] = y.astype(BF)

    return call(
        kernel,
        (rows // tile,),
        [group_blocks(tile, width, g, per) for g in range(count)]
        + [pl.BlockSpec((width, cols), lambda i, c: (0, c[0]), pipeline_mode=pl.Buffered(1))]
        + [whole((1, TILE))] * 2 + [row_blocks(tile, TILE)] * 2,
        [row_blocks(tile, q_cols), row_blocks(tile, 2 * kv_cols), row_blocks(tile, raw_cols)],
        [shaped((rows, q_cols), BF), shaped((rows, 2 * kv_cols), BF), shaped((rows, raw_cols), F32)],
        "project_heads",
        scalars=[core],
    )(*groups, weight_all, q_gain, k_gain, cos, sin)


def head_grads(parts, raw, first_tile, heads, gain, cos, sin):
    rows, cols = parts[0].shape
    normed = (heads + 1) // 2
    count, tile = len(parts), 256

    def kernel(*refs):
        ds, (raw_ref, gain_ref, cos_ref, sin_ref, g_ref, sum_ref) = refs[:count], refs[count:]
        lane = lane_of((tile, TILE))
        even, first = lane < HEAD_SIZE, lane % HEAD_SIZE < HEAD_SIZE // 2
        cos, sin, gain = cos_ref[...], sin_ref[...], gain_ref[...]

        @pl.when(pl.program_id(0) == 0)
        def _():
            sum_ref[...] = jnp.zeros_like(sum_ref)

        for t in range(cols // TILE):
            at = slice(t * TILE, (t + 1) * TILE)
            d = sum(ref[:, at].astype(F32) for ref in ds)
            y = d
            if t < normed:
                x = raw_ref[:, at]
                r = lax.rsqrt(half_sums(x * x, even) * (1.0 / HEAD_SIZE) + EPS)
                n = x * r
                back = d * cos - turned(d, first) * sin
                dn = back * n
                w = back * gain
                y = r * (w - n * (half_sums(w * n, even) * (1.0 / HEAD_SIZE)))
                if heads - 2 * t == 1:
                    y = jnp.where(even, y, d)
                    dn = jnp.where(even, dn, 0.0)
                sum_ref[...] += jnp.sum(dn.reshape(tile // 8, 8, TILE), axis=0)
            g_ref[:, at] = y.astype(BF)

    raw_at = first_tile // normed
    return call(
        kernel,
        (rows // tile,),
        [row_blocks(tile, cols)] * count
        + [pl.BlockSpec((tile, normed * TILE), lambda i: (i, raw_at)), whole((1, TILE))]
        + [row_blocks(tile, TILE)] * 2,
        [row_blocks(tile, cols), whole((8, TILE))],
        [shaped((rows, cols), BF), shaped((8, TILE), F32)],
        "head_grads",
    )(*parts, raw, gain, cos, sin)


def stacked(ref, g, even):
    out = []
    for p in range(2):
        pair = ref[0, :, (2 * g + p) * TILE : (2 * g + p + 1) * TILE]
        zero = jnp.zeros_like(pair)
        out += [jnp.where(even, pair, zero), jnp.where(even, zero, pair)]
    return jnp.concatenate(out, axis=0)


def unstacked(values, p, even):
    base = 2 * p * TILE
    return jnp.where(even, values[base : base + TILE], values[base + TILE : base + 2 * TILE])


def widen(refs, k_ref, v_ref, heads):
    at = 0
    for ref in refs:
        for r in range(0, ref.shape[1], TILE):
            rows = slice(at, at + TILE)
            lane = lane_of((TILE, TILE))
            even = lane < HEAD_SIZE
            for t in range(heads):
                x = ref[0, r : r + TILE, t * TILE : (t + 1) * TILE].astype(F32)
                other = pltpu.roll(x, HEAD_SIZE, 1)
                for part, value in enumerate((jnp.where(even, x, other), jnp.where(even, other, x))):
                    n = 2 * t + part
                    out = k_ref if n < heads else v_ref
                    out[rows, (n % heads) * TILE : (n % heads + 1) * TILE] = value.astype(BF)
            at += TILE


def narrow(k_ref, v_ref, rows, t, heads, even):
    tiles = []
    for n in (2 * t, 2 * t + 1):
        ref, scale = (k_ref, SCALE) if n < heads else (v_ref, 1.0)
        x = ref[rows, (n % heads) * TILE : (n % heads + 1) * TILE]
        tiles.append((x + pltpu.roll(x, HEAD_SIZE, 1)) * scale)
    return jnp.where(even, tiles[0], tiles[1])


def attend(low_block, q, kv_prior, kv, qseg, kseg):
    batch, rows, cols = q.shape
    blocks = rows // TILE
    heads = kv.shape[2] // TILE
    keys = 2 * rows

    def kernel(lo_ref, q_ref, prior_ref, kv_ref, qseg_ref, kseg_ref, o_ref, lse_ref, acc_ref, sum_ref, k_ref, v_ref):
        b, i = pl.program_id(0), pl.program_id(1)
        lane = lane_of((TILE, TILE))
        even = lane < HEAD_SIZE

        @pl.when(i == 0)
        def _():
            widen((prior_ref, kv_ref), k_ref, v_ref, heads)

        qs = [stacked(q_ref, g, even) for g in range(heads)]
        acc_ref[...] = jnp.zeros_like(acc_ref)
        sum_ref[...] = jnp.zeros_like(sum_ref)
        seg = qseg_ref[0]
        row_at = lax.broadcasted_iota(jnp.int32, (TILE, TILE), 0) + (i + blocks) * TILE

        def step(j, carry):
            at = pl.ds(pl.multiple_of(j * TILE, TILE), TILE)
            ok = (seg == kseg_ref[0, pl.ds(j, 1), :]) & (lane + j * TILE <= row_at)
            bias = jnp.where(ok, 0.0, -1e30)
            bias = jnp.concatenate([bias] * 4, axis=0)
            for g in range(heads):
                col = slice(g * TILE, (g + 1) * TILE)
                e = jnp.exp(dot_nt(qs[g], k_ref[at, col]) * SCALE + bias)
                sum_ref[g] += e
                acc_ref[g] += dot(e.astype(BF), v_ref[at, col])
            return carry

        lax.fori_loop(lo_ref[b * blocks + i], i + blocks + 1, step, 0)
        lse = jnp.zeros((TILE, TILE), F32)
        for g in range(heads):
            total = jnp.sum(sum_ref[g], axis=-1, keepdims=True)
            out = acc_ref[g] / total
            log = jnp.log(total)
            for p in range(2):
                o_ref[0, :, (2 * g + p) * TILE : (2 * g + p + 1) * TILE] = unstacked(out, p, even).astype(BF)
            for h in range(4):
                lse = jnp.where(lane == 4 * g + h, log[h * TILE : (h + 1) * TILE], lse)
        lse_ref[0] = lse

    per_q = lambda n: pl.BlockSpec((1, TILE, n), lambda b, i, lo: (b, i, 0))
    per_b = lambda s: pl.BlockSpec((1,) + s[1:], lambda b, i, lo: (b, 0, 0))
    return call(
        kernel,
        (batch, blocks),
        [per_q(cols), per_b(kv.shape), per_b(kv.shape), per_q(1), per_b(kseg.shape)],
        [per_q(cols), per_q(TILE)],
        [shaped(q.shape, BF), shaped((batch, rows, TILE), F32)],
        "attend",
        [pltpu.VMEM((heads, 4 * TILE, TILE), F32)] * 2 + [pltpu.VMEM((keys, heads * TILE), BF)] * 2,
        [low_block],
    )(q, kv_prior, kv, qseg, kseg)


def attend_back(low_block, q, kv_prior, kv, qseg, kseg, o, lse, do):
    batch, rows, cols = q.shape
    blocks = rows // TILE
    heads = kv.shape[2] // TILE
    keys = 2 * rows

    def kernel(lo_ref, q_ref, prior_ref, kv_ref, qseg_ref, kseg_ref, o_ref, lse_ref, do_ref, dq_ref, dprior_ref, dkv_ref, acc_ref, k_ref, v_ref, dk_ref, dv_ref):
        b, i = pl.program_id(0), pl.program_id(1)
        lane = lane_of((TILE, TILE))
        even = lane < HEAD_SIZE

        @pl.when(i == 0)
        def _():
            widen((prior_ref, kv_ref), k_ref, v_ref, heads)
            dk_ref[...] = jnp.zeros_like(dk_ref)
            dv_ref[...] = jnp.zeros_like(dv_ref)

        qs = [stacked(q_ref, g, even) for g in range(heads)]
        dos = [stacked(do_ref, g, even) for g in range(heads)]
        lses, deltas = [], []
        for g in range(heads):
            os = stacked(o_ref, g, even)
            deltas.append(jnp.sum(os.astype(F32) * dos[g].astype(F32), axis=-1, keepdims=True))
            each = [
                jnp.sum(jnp.where(lane == 4 * g + h, lse_ref[0], 0.0), axis=-1, keepdims=True)
                for h in range(4)
            ]
            lses.append(jnp.concatenate(each, axis=0))
        acc_ref[...] = jnp.zeros_like(acc_ref)
        seg = qseg_ref[0]
        row_at = lax.broadcasted_iota(jnp.int32, (TILE, TILE), 0) + (i + blocks) * TILE

        def step(j, carry):
            at = pl.ds(pl.multiple_of(j * TILE, TILE), TILE)
            ok = (seg == kseg_ref[0, pl.ds(j, 1), :]) & (lane + j * TILE <= row_at)
            bias = jnp.where(ok, 0.0, -1e30)
            bias = jnp.concatenate([bias] * 4, axis=0)
            for g in range(heads):
                col = slice(g * TILE, (g + 1) * TILE)
                k, v = k_ref[at, col], v_ref[at, col]
                p = jnp.exp(dot_nt(qs[g], k) * SCALE + (bias - lses[g]))
                ds = (p * (dot_nt(dos[g], v) - deltas[g])).astype(BF)
                dv_ref[at, col] += dot_tn(p.astype(BF), dos[g])
                dk_ref[at, col] += dot_tn(ds, qs[g])
                acc_ref[g] += dot(ds, k)
            return carry

        lax.fori_loop(lo_ref[b * blocks + i], i + blocks + 1, step, 0)
        for g in range(heads):
            for p in range(2):
                dq_ref[0, :, (2 * g + p) * TILE : (2 * g + p + 1) * TILE] = (
                    unstacked(acc_ref[g], p, even) * SCALE
                )

        @pl.when(i == blocks - 1)
        def _():
            for r in range(0, rows, TILE):
                for t in range(heads):
                    col = slice(t * TILE, (t + 1) * TILE)
                    dprior_ref[0, r : r + TILE, col] = narrow(
                        dk_ref, dv_ref, slice(r, r + TILE), t, heads, even
                    ).astype(BF)
                    dkv_ref[0, r : r + TILE, col] = narrow(
                        dk_ref, dv_ref, slice(rows + r, rows + r + TILE), t, heads, even
                    )

    per_q = lambda n: pl.BlockSpec((1, TILE, n), lambda b, i, lo: (b, i, 0))
    per_b = lambda s: pl.BlockSpec((1,) + s[1:], lambda b, i, lo: (b, 0, 0))
    wide = (keys, heads * TILE)
    return call(
        kernel,
        (batch, blocks),
        [per_q(cols), per_b(kv.shape), per_b(kv.shape), per_q(1), per_b(kseg.shape)]
        + [per_q(cols), per_q(TILE), per_q(cols)],
        [per_q(cols), per_b(kv.shape), per_b(kv.shape)],
        [shaped(q.shape, F32), shaped(kv.shape, BF), shaped(kv.shape, F32)],
        "attend_back",
        [pltpu.VMEM((heads, 4 * TILE, TILE), F32)]
        + [pltpu.VMEM(wide, BF)] * 2 + [pltpu.VMEM(wide, F32)] * 2,
        [low_block],
    )(q, kv_prior, kv, qseg, kseg, o, lse, do)


def hidden_units(hidden, low, gate_up, down):
    half, width = hidden[0].shape
    cols = down.shape[0]
    tile = 256
    per = half // tile
    count = len(hidden)

    def kernel(*refs):
        hid, lows = refs[:count], refs[count : 2 * count]
        gu_ref, wd_ref, act_ref, grad_ref = refs[2 * count :]
        x, y = pick_group(hid, per), pick_group(lows, per)
        step = 256
        for c in range(0, cols, step):
            n = min(step, cols - c)
            gate = dot(x, gu_ref[:, c : c + n])
            up = dot(x, gu_ref[:, cols + c : cols + c + n])
            grad = dot_nt(y, wd_ref[c : c + n, :])
            sig = 1.0 / (1.0 + jnp.exp(-gate))
            silu = gate * sig
            act_ref[:, c : c + n] = (silu * up).astype(BF)
            grad_ref[:, c : c + n] = (grad * up * (sig * (1.0 + gate * (1.0 - sig)))).astype(BF)
            grad_ref[:, cols + c : cols + c + n] = (grad * silu).astype(BF)

    groups = [group_blocks(tile, width, g, per) for g in range(count)]
    rows = count * half
    return call(
        kernel,
        (rows // tile,),
        groups + groups + [once(gate_up.shape), once(down.shape)],
        [row_blocks(tile, cols), row_blocks(tile, 2 * cols)],
        [shaped((rows, cols), BF), shaped((rows, 2 * cols), BF)],
        "hidden_units",
    )(*hidden, *low, gate_up, down)


def tall_grad(groups, rights, bit, name):
    half, width = groups[0].shape
    cols = rights[0].shape[1]
    count, pairs = len(groups), len(rights)
    tile = 512
    steps = width // tile
    split = bit is not None
    side = steps // 2 if split else 0

    def kernel(bit_ref, *refs):
        lefts, right, outs = refs[:count], refs[count : count + pairs], refs[count + pairs :]
        total = None
        for g in range(count):
            r = right[g // 2][(g % 2) * half : (g % 2 + 1) * half, :]
            term = dot_tn(lefts[g][...], r)
            total = term if total is None else total + term

        @pl.when(pl.program_id(0) >= side)
        def _():
            outs[0][...] = total.astype(BF)

        if split:

            @pl.when(pl.program_id(0) < side)
            def _():
                outs[1][...] = total.astype(BF)

    def column(i, bit):
        if not split:
            return (0, i)
        return (0, i % side + side * jnp.where(i >= side, bit[0], 1 - bit[0]))

    out_specs = [pl.BlockSpec((tile, cols), lambda i, b: (jnp.maximum(i - side, 0), 0))]
    if split:
        out_specs.append(pl.BlockSpec((tile, cols), lambda i, b: (jnp.minimum(i, side - 1), 0)))
    return call(
        kernel,
        (steps,),
        [pl.BlockSpec((half, tile), column)] * count + [once(r.shape) for r in rights],
        out_specs,
        [shaped(((steps - side) * tile, cols), BF)] * len(out_specs),
        name,
        scalars=[bit if split else 0],
    )(*groups, *rights)


def wide_grad(lefts, groups, name):
    half, width = groups[0].shape
    cols = lefts[0].shape[1]
    count, pairs = len(groups), len(lefts)
    tile = 512

    def kernel(*refs):
        total = None
        for g in range(count):
            left = refs[g // 2][(g % 2) * half : (g % 2 + 1) * half, :]
            term = dot_tn(left, refs[pairs + g][...])
            total = term if total is None else total + term
        refs[-1][...] = total.astype(BF)

    return call(
        kernel,
        (width // tile,),
        [once(a.shape) for a in lefts] + [pl.BlockSpec((half, tile), lambda i: (0, i))] * count,
        pl.BlockSpec((cols, tile), lambda i: (0, i)),
        shaped((cols, width), BF),
        name,
    )(*lefts, *groups)


def sum_products(lefts, rights, transposed, name, core=0, part=None):
    rows = lefts[0].shape[0]
    width = rights[0].shape[0] if transposed else rights[0].shape[1]
    tile, count = 512, len(lefts)

    def kernel(core_ref, *refs):
        total = None
        for a, b in zip(refs[:count], refs[count : 2 * count]):
            term = dot_nt(a[...], b[...]) if transposed else dot(a[...], b[...])
            total = term if total is None else total + term
        refs[-2][...] = total[: rows // 2]
        refs[-1][...] = total[rows // 2 :].astype(BF)

    at = lambda c: c[0] if part else 0
    if transposed:
        right = [
            pl.BlockSpec((tile, part or r.shape[1]), lambda i, c: (i, at(c))) for r in rights
        ]
    else:
        right = [
            pl.BlockSpec((part or r.shape[0], tile), lambda i, c: (at(c), i)) for r in rights
        ]
    column = pl.BlockSpec((rows // 2, tile), lambda i, c: (0, i))
    return call(
        kernel,
        (width // tile,),
        [once(a.shape) for a in lefts] + right,
        [column, column],
        [shaped((rows // 2, width), F32), shaped((rows // 2, width), BF)],
        name,
        scalars=[core],
    )(*lefts, *rights)


def first_sum(grad_q, grad_kv, weights, core):
    rows, part = grad_kv.shape
    width, tile = weights.shape[0], 512
    count = grad_q.shape[1] // part + 1

    def kernel(core_ref, *refs):
        total = None
        for a, b in zip(refs[:count], refs[count : 2 * count]):
            term = dot_nt(a[...], b[...])
            total = term if total is None else total + term
        refs[-2][...] = total[: rows // 2]
        refs[-1][...] = total[rows // 2 :].astype(BF)

    column_of = lambda n: pl.BlockSpec(
        (rows, part), lambda i, c: (0, n), pipeline_mode=pl.Buffered(1)
    )
    weight_of = lambda n: pl.BlockSpec((tile, part), lambda i, c: (i, count * c[0] + n))
    column = pl.BlockSpec((rows // 2, tile), lambda i, c: (0, i))
    return call(
        kernel,
        (width // tile,),
        [column_of(n) for n in range(count - 1)] + [column_of(0)]
        + [weight_of(n) for n in range(count)],
        [column, column],
        [shaped((rows // 2, width), F32), shaped((rows // 2, width), BF)],
        "first_sum",
        scalars=[core],
    )(*[grad_q] * (count - 1), grad_kv, *[weights] * count)


def token_product(groups, weight, core, part, name):
    half, width = groups[0].shape
    tile = 256
    per, count = half // tile, len(groups)

    def kernel(core_ref, *refs):
        refs[-1][...] = dot_nt(pick_group(refs[:count], per), refs[count][...]).astype(BF)

    return call(
        kernel,
        (count * per,),
        [group_blocks(tile, width, g, per) for g in range(count)]
        + [pl.BlockSpec((part, width), lambda i, c: (c[0], 0), pipeline_mode=pl.Buffered(1))],
        row_blocks(tile, part),
        shaped((count * half, part), BF),
        name,
        scalars=[core],
    )(*groups, weight)


def unit_moves(groups, size, pieces, padded):
    moves = []
    for n in range(2):
        for j, (a, b) in enumerate(pieces):
            for owner in range(4 * groups):
                at = ((2 * j + n) * groups + owner // 4) * padded
                moves.append((n, owner % 4, owner * size + a, at, b - a))
    return moves


def split_units(gate, up, groups, size, pieces, padded):
    rows, cols = gate.shape
    moves = unit_moves(groups, size, pieces, padded)
    share = 2 * len(pieces) * groups * padded

    def kernel(gate_ref, up_ref, out_ref, wide, kinds):
        kinds[...] = jnp.zeros_like(kinds)
        for n, ref in enumerate((gate_ref, up_ref)):
            wide[...] = ref[...].astype(F32)
            for m, c, src, dst, width in moves:
                if m == n:
                    kinds[c, :, dst : dst + width] = wide[:, src : src + width]
        out_ref[...] = kinds[...].astype(BF)

    out = shaped((4, rows, share), BF)
    return call(
        kernel,
        (1,),
        [whole((rows, cols))] * 2,
        whole(out.shape),
        out,
        "split_units",
        [pltpu.VMEM((rows, cols), F32), pltpu.VMEM(out.shape, F32)],
    )(gate, up)


def join_units(classes, groups, size, pieces, padded):
    rows = classes[0].shape[0]
    moves = unit_moves(groups, size, pieces, padded)

    def kernel(a_ref, b_ref, c_ref, d_ref, gate_ref, up_ref):
        for n, c, src, dst, width in moves:
            ref = (a_ref, b_ref, c_ref, d_ref)[c]
            (gate_ref, up_ref)[n][:, src : src + width] = ref[:, dst : dst + width]

    out = shaped((rows, 4 * groups * size), F32)
    return call(
        kernel,
        (1,),
        [whole(classes[0].shape)] * 4,
        [whole(out.shape)] * 2,
        [out] * 2,
        "join_units",
    )(*classes)


QUERY_HEADS = 24
KEY_VALUE_HEADS = 6
AXES = ("seq", "z", "x", "core")
CHUNKS = 2
UNITS, DOWN, OUT, QKV = range(4)
PLAN = {
    (UNITS, 0): (0, 1, 2),
    (DOWN, 0): (0, 1, 2),
    (UNITS, 1): (1, 2, 3),
    (DOWN, 1): (2, 3, 4),
    (DOWN, 0, True): (5, 6, 7),
    (UNITS, 0, True): (5, 6, 7),
    (DOWN, 1, True): (6, 7, 8),
    (UNITS, 1, True): (7, 8, 9),
    (OUT, 0, True): (9, 10, 11, 12),
    (OUT, 1, True): (9, 10, 11, 12),
    (QKV, 0, True): (11, 12, 13, 14),
    (QKV, 1, True): (12, 13, 14, 15),
}


def swap_core(value):
    return lax.ppermute(value, "core", [(0, 1), (1, 0)])


def core_pick(first, second):
    return jnp.where(lax.axis_index("core") == 0, first, second)


def core_concat(own, other, axis=0):
    return core_pick(
        jnp.concatenate([own, other], axis=axis), jnp.concatenate([other, own], axis=axis)
    )


def swap_seq(value):
    return lax.ppermute(value, "seq", [(0, 1), (1, 0)])


def swap_x(value):
    return lax.ppermute(value, "x", [(0, 1), (1, 0)])


def x_pick(first, second):
    return jnp.where(lax.axis_index("x") == 0, first, second)


def group_axes():
    bits = lax.axis_size("z").bit_length() - 1
    return [("seq", 1)] + [("z", 1 << k) for k in reversed(range(bits))]


def orders_of(name):
    cube = group_axes()
    far, near, seq = cube[1:-1], cube[-1:], cube[:1]
    what, number = name[:2]
    if what in (OUT, QKV):
        x = [("x", 1)]
        cube = cube + x
        stages = [far, seq, near, x] if number else [far, x, near, seq]
    else:
        stages = [far, seq, near] if what == DOWN else [far, near, seq]
    return cube, [s[::-1] for s in stages[::-1]] if len(name) > 2 else stages


def hop_bit(hop):
    axis, step = hop
    return lax.axis_index(axis) // step % 2


def exchange(value, hop):
    axis, step = hop
    return lax.ppermute(value, axis, [(i, i ^ step) for i in range(lax.axis_size(axis))])


def place_kernel(bit_ref, own_ref, got_ref, out_ref):
    bit = bit_ref[0]
    out_ref[:, pl.ds(bit, 1)] = own_ref[...][:, None]
    out_ref[:, pl.ds(1 - bit, 1)] = got_ref[...][:, None]


def placed(own, got, dim, bit):
    shape = own.shape
    lead, inner = math.prod(shape[:dim]), math.prod(shape[dim:-2])
    flat = (lead, inner) + shape[-2:]
    part = math.gcd(inner, 2) if lead == 1 else inner
    block = (1, part) + shape[-2:]
    side = pl.BlockSpec(block, lambda i, j, bit: (i, j, 0, 0))
    out = call(
        place_kernel,
        (lead, inner // part),
        [side, side],
        pl.BlockSpec((1, 2) + block[1:], lambda i, j, bit: (i, 0, j, 0, 0)),
        shaped((lead, 2) + flat[1:], own.dtype),
        "place",
        scalars=[bit],
    )(own.reshape(flat), got.reshape(flat))
    return out.reshape(shape[:dim] + (2,) + shape[dim + 1 :])


class Values:
    def __init__(self):
        for name in ("low", "hidden", "wgu", "wd", "act", "ggu", "keep", "home"):
            setattr(self, name, {})


class Flow:
    def __init__(self):
        self.live = Values()
        self.rest, self.flight, self.later, self.stage, self.now = {}, {}, {}, {}, 0

    def fence(self):
        values, parts = lax.optimization_barrier((vars(self.live), self.rest))
        vars(self.live).update(values)
        self.rest = parts

    def gather(self, name, block):
        self.rest[name] = block.reshape((1,) * len(orders_of(name)[0]) + block.shape)
        self.stage[name] = 0

    def scatter(self, name, rows, grad, sent=None):
        self.stage[name] = 0
        shape = [2] * len(orders_of(name)[0])
        if sent is None:
            self.rest[name] = grad.reshape(shape + [rows, grad.shape[1]])
        else:
            shape[self.hop(name)[1]] = 1
            self.rest[name] = tuple(v.reshape(shape + [rows, v.shape[1]]) for v in (grad, sent))

    def hop(self, name):
        cube, stages = orders_of(name)
        hop = sum(stages, [])[self.stage[name]]
        return hop, cube.index(hop)

    def start(self, name):
        hop, dim = self.hop(name)
        bit, value = hop_bit(hop), self.rest.pop(name)
        if isinstance(value, tuple):
            value, sent = value
        elif len(name) > 2:
            sent = lax.dynamic_slice_in_dim(value, 1 - bit, 1, dim)
        else:
            sent = value
        self.flight[name] = (value, exchange(sent, hop), dim, bit)

    def land(self, name):
        keep, got, dim, bit = self.flight.pop(name)
        self.stage[name] += 1
        stages = orders_of(name)[1]
        ends = [sum(map(len, stages[: k + 1])) for k in range(len(stages))]
        last = self.stage[name] == ends[-1]
        if len(name) > 2:
            if keep.shape[dim] == 2:
                keep = lax.dynamic_slice_in_dim(keep, bit, 1, dim)
            total = keep.astype(F32) + got.astype(F32)
            self.rest[name] = total if last else total.astype(BF)
        elif last:
            self.rest[name] = (keep, got)
            self.stage[name] = (dim, bit)
        else:
            self.rest[name] = placed(keep, got, dim, bit)
        if not last and self.stage[name] not in ends:
            self.start(name)
            self.land(name)

    def take(self, name):
        value = self.rest.pop(name)
        dims = len(orders_of(name)[0])
        if len(name) > 2:
            return value.reshape(value.shape[dims:])
        value = placed(*value, *self.stage[name])
        return value.reshape((-1,) + value.shape[dims + 1 :])

    def post(self, value, name, key=None, wait=0):
        self.later[name, key] = (value, self.now + wait)

    def interval(self, *work):
        active = [name for name, at in PLAN.items() if self.now in at]
        for name in active:
            self.start(name)
        for piece in work:
            piece()
        for name in active:
            self.land(name)
        for name, key in [n for n, (_, at) in self.later.items() if at == self.now]:
            value = self.later.pop((name, key))[0]
            if key is None:
                setattr(self.live, name, value)
            else:
                getattr(self.live, name)[key] = value
        self.fence()
        self.now += 1


def row_norm(values):
    scale = lax.rsqrt(jnp.mean(values * values, axis=-1, keepdims=True) + EPS)
    return values * scale, scale


def norm_back(grad, normed, scale, gain):
    u = grad * gain
    return scale * (u - normed * jnp.mean(u * normed, axis=-1, keepdims=True))


def doc_positions(segment_row):
    length = segment_row.shape[-1]
    places = jnp.arange(length, dtype=jnp.int32)
    earlier = jnp.concatenate([segment_row[..., :1] + 1, segment_row[..., :-1]], axis=-1)
    starts = jnp.where(segment_row != earlier, places, 0)
    latest = jnp.max(
        jnp.where(places[None, :] <= places[:, None], starts[..., None, :], 0), axis=-1
    )
    return places - latest


def rotary_tables(positions):
    pair_count = HEAD_SIZE // 2
    frequencies = jnp.exp(
        jnp.arange(pair_count, dtype=F32) * (-2.0 * math.log(10000.0) / HEAD_SIZE)
    )
    phases = positions.astype(F32)[..., None] * frequencies
    cos, sin = jnp.cos(phases), jnp.sin(phases)
    return jnp.tile(cos, (1, 4)), jnp.tile(jnp.concatenate([-sin, sin], axis=1), (1, 2))


def split_rows(rows, pieces):
    units, rest = rows // 8, rows % 8
    sizes = [8 * (units // pieces + (i < units % pieces)) for i in range(pieces)]
    sizes[-1] += rest
    ends = [sum(sizes[: i + 1]) for i in range(pieces)]
    return [(e - s, e) for s, e in zip(sizes, ends)]


def halves(w):
    n = w.shape[1] // 2
    return w[:, :n], w[:, n:]


def body(
    tokens,
    segments,
    attn_gain,
    w_query,
    key_projection_weight,
    value_projection_weight,
    query_norm_gain,
    key_gain,
    w_out,
    ffn_gain,
    w_gate,
    w_up,
    w_down,
    cotangent,
):
    _, half, width = tokens.shape
    ny, nz, nx = (lax.axis_size(a) for a in ("seq", "z", "x"))
    groups = ny * nz
    core, seq, x_at = (lax.axis_index(a) for a in ("core", "seq", "x"))
    q_cols, kv_cols = w_query.shape[1] // 2, key_projection_weight.shape[1] // 2
    kv_heads = KEY_VALUE_HEADS // 2
    out_rows, ff_rows, in_rows = w_out.shape[0], w_down.shape[0], w_gate.shape[0]
    pieces = split_rows(ff_rows, CHUNKS)
    step = TILE // math.gcd(TILE, groups)
    padded = -(-max(b - a for a, b in pieces) // step) * step
    share = groups * padded
    flow = Flow()
    do = lambda f, *a: (lambda: f(*a))

    def pair(value):
        return [value, swap_core(value)]

    def trade(value):
        return lax.ppermute(value, ("seq", "core"), [(0, 0), (1, 2), (2, 1), (3, 3)])

    weights = (w_query, key_projection_weight, value_projection_weight)
    lows, highs = zip(*(halves(w) for w in weights))
    gains = jnp.pad(jnp.stack([attn_gain, ffn_gain], axis=1), ((0, 0), (0, TILE - 2)))
    qkv_all = lax.all_gather(
        jnp.concatenate(lows + highs + (gains,), axis=1), AXES, axis=0, tiled=True
    )

    quarters = split_units(w_gate, w_up, groups, ff_rows, pieces, padded)
    mine = [core_pick(quarters[2 * x], quarters[2 * x + 1]) for x in range(2)]
    theirs = [core_pick(quarters[2 * x + 1], quarters[2 * x]) for x in range(2)]
    sent = x_pick(jnp.concatenate(theirs), jnp.concatenate(theirs[::-1]))
    got = swap_core(sent)
    near = core_concat(x_pick(mine[0], mine[1]), got[:in_rows])
    far = swap_x(core_concat(x_pick(mine[1], mine[0]), got[in_rows:]))
    block = x_pick(jnp.concatenate([near, far]), jnp.concatenate([far, near]))
    live = flow.live
    for j, (a, b) in enumerate(pieces):
        units_block = block[:, 2 * j * share : 2 * (j + 1) * share]
        down_block = jnp.pad(w_down[a:b], ((0, padded - b + a), (0, 0)))
        flow.gather((UNITS, j), units_block)
        flow.gather((DOWN, j), down_block)
    live.w_out = w_out
    pending = {}

    def gather_qkv():
        flow.live.qkv = qkv_all

    def gather_out():
        pending[OUT] = lax.all_gather(flow.live.w_out, AXES, axis=0, tiled=True)

    def tables():
        live = flow.live
        segments_pair = jnp.concatenate(pair(segments), axis=0)
        positions = doc_positions(segments_pair)
        own_start = seq * half
        own_positions = lax.dynamic_slice_in_dim(positions, own_start, half, 1)
        order_ids = jnp.where(segments_pair < 0, 1 << 20, segments_pair)
        own_ids = lax.dynamic_slice_in_dim(order_ids, own_start, half, 1)
        prior_ids = lax.dynamic_slice_in_dim(order_ids, jnp.maximum(own_start - half, 0), half, 1)
        prior_ids = jnp.where(own_start >= half, prior_ids, -2)
        key_ids = jnp.concatenate([prior_ids, own_ids], axis=1)
        low_block = jnp.sum(key_ids[:, None, :] < own_ids[:, ::TILE, None], axis=-1) // TILE
        live.low_block = low_block.astype(jnp.int32)
        live.query_ids = own_ids[:, :, None]
        live.key_ids = key_ids.reshape(2, -1, TILE)
        live.cos, live.sin = rotary_tables(own_positions.reshape(2 * half))
        live.q_gain = jnp.tile(query_norm_gain.astype(F32), 2).reshape(1, TILE)
        live.k_gain = jnp.tile(key_gain.astype(F32), 2).reshape(1, TILE)

    def first_norm():
        live = flow.live
        live.low[0] = pair(cotangent.reshape(half, width))
        live.normed, live.scale = row_norm(tokens.reshape(half, width).astype(F32))

    def far_low():
        flow.post(swap_x(flow.live.low[0][0]), "far_low")

    def near_low():
        flow.live.low[1] = pair(flow.live.far_low)

    def heads():
        live = flow.live
        n = q_cols + 2 * kv_cols
        live.gains = live.qkv[:, 2 * n : 2 * n + 2].T.astype(F32)
        live.hidden_first = pair((live.normed * live.gains[0]).astype(BF))
        q_rot, kv, live.raw = project(
            live.hidden_first, live.qkv, core, live.q_gain, live.k_gain, live.cos,
            live.sin, q_cols, kv_cols,
        )
        live.q, live.kv = q_rot.reshape(2, half, -1), kv.reshape(2, half, -1)
        flow.post(swap_seq(live.kv), "prior_kv")

    def attention():
        live = flow.live
        attn, live.lse = attend(
            live.low_block, live.q, live.prior_kv, live.kv, live.query_ids,
            live.key_ids,
        )
        live.attn = attn.reshape(2 * half, q_cols)

    def near_rows(sums):
        return sums[0] + swap_core(sums[1]).astype(F32)

    def branch():
        live = flow.live
        live.out = pending.pop(OUT)
        term = near_rows(
            sum_products([live.attn], [live.out], False, "branch", core, q_cols)
        )
        live.middle = tokens.reshape(half, width).astype(F32) + term
        live.normed2, live.scale2 = row_norm(live.middle)
        hidden = (live.normed2 * live.gains[1]).astype(BF)
        live.hidden[0] = pair(hidden)

    def far_hidden():
        flow.post(swap_x(flow.live.hidden[0][0]), "far_hidden")

    def near_hidden():
        flow.live.hidden[1] = pair(flow.live.far_hidden)

    def units(j, h):
        live = flow.live
        if h == 0:
            live.wgu[j], live.wd[j] = flow.take((UNITS, j)), flow.take((DOWN, j))
        live.act[j, h], live.ggu[j, h] = hidden_units(
            live.hidden[h], live.low[h], live.wgu[j], live.wd[j]
        )

    def down_grad(j):
        live = flow.live
        acts = [live.act[j, h] for h in range(2)]
        grad = wide_grad(acts, live.low[0] + live.low[1], "down_grad")
        flow.scatter((DOWN, j, True), padded, grad)

    def units_grad(j):
        live = flow.live
        grads = [live.ggu[j, h] for h in range(2)]
        grads = tall_grad(live.hidden[0] + live.hidden[1], grads, seq, "units_grad")
        flow.scatter((UNITS, j, True), 4 * in_rows, *grads)

    def hidden_sum(h):
        live = flow.live
        js = range(CHUNKS)
        total = near_rows(
            sum_products(
                [live.ggu[j, h] for j in js], [live.wgu[j] for j in js], True, "hidden_sum"
            )
        )
        if h:
            live.far_grad_sum = total.astype(BF)
        else:
            live.near_grad = total

    def far_grad():
        flow.post(swap_x(flow.live.far_grad_sum), "far_grad")

    def down_sum(h):
        live = flow.live
        js = range(CHUNKS)
        total = near_rows(
            sum_products(
                [live.act[j, h] for j in js], [live.wd[j] for j in js], False, "down_sum"
            )
        )
        if h:
            live.far_result_sum = total.astype(BF)
        else:
            live.near_result = total

    def far_result():
        flow.post(swap_x(flow.live.far_result_sum), "far_result")

    def second_back():
        live = flow.live
        grad = live.near_grad + live.far_grad.astype(F32)
        live.grad_middle = cotangent.reshape(half, width).astype(F32) + norm_back(
            grad, live.normed2, live.scale2, live.gains[1]
        )
        live.grad_branch = pair(live.grad_middle.astype(BF))

    def out_grad():
        live = flow.live
        live.grad_attn = token_product(
            live.grad_branch, live.out, core, q_cols, "grad_attn"
        )
        grad = wide_grad([live.attn], live.grad_branch, "out_grad")
        grad = grad.reshape(nz * nx, 2, out_rows, width).transpose(1, 0, 2, 3)
        grad = grad.reshape(groups * nx * out_rows, width)
        flow.scatter((OUT, 0, True), out_rows, grad[:, : width // 2])
        flow.scatter((OUT, 1, True), out_rows, grad[:, width // 2 :])

    def attention_back():
        live = flow.live
        dq, live.sent_dkv, live.dkv = attend_back(
            live.low_block, live.q, live.prior_kv, live.kv, live.query_ids,
            live.key_ids, live.attn.reshape(2, half, q_cols), live.lse,
            live.grad_attn.reshape(2, half, q_cols),
        )
        live.dq = dq.reshape(2 * half, q_cols)

    def prior_back():
        flow.post(swap_seq(flow.live.sent_dkv), "prior_dkv")

    def queries_back():
        live = flow.live
        live.grad_q, live.q_part = head_grads(
            [live.dq], live.raw, 0, q_cols // HEAD_SIZE, live.q_gain, live.cos, live.sin
        )
        grads = tall_grad(live.hidden_first, [live.grad_q], seq, "q_grad")
        flow.scatter((QKV, 0, True), 2 * in_rows, *grads)

    def keys_back():
        live = flow.live
        tall = lambda v: v.reshape(2 * half, -1)
        live.grad_kv, k_part = head_grads(
            [tall(live.dkv), tall(live.prior_dkv)], live.raw, q_cols // TILE,
            kv_cols // HEAD_SIZE, live.k_gain, live.cos, live.sin,
        )
        grad = tall_grad(live.hidden_first, [live.grad_kv], None, "kv_grad")
        flow.scatter((QKV, 1, True), 2 * in_rows, grad[0])
        parts = jnp.stack([live.q_part, k_part]).sum(axis=1)
        live.head_gains = parts.reshape(2, 2, HEAD_SIZE).sum(axis=1)

    def first_back():
        live = flow.live
        grad = near_rows(first_sum(live.grad_q, live.grad_kv, live.qkv, core))
        live.input_grad = live.grad_middle + norm_back(
            grad, live.normed, live.scale, live.gains[0]
        )

    def finish_output():
        live = flow.live
        total = live.near_result + live.far_result.astype(F32)
        live.output = (live.middle + total).astype(BF)

    def gain_hops(hops):
        for hop in hops:
            flow.live.head_gains = flow.live.head_gains + exchange(flow.live.head_gains, hop)

    def home(j):
        rows = flow.take((UNITS, j, True)).reshape(2, 2 * in_rows, -1)
        flow.live.keep[j] = x_pick(rows[0], rows[1])
        flow.post(swap_x(x_pick(rows[1], rows[0])), "home", j)

    def own_shard(block):
        block = block.reshape(2, in_rows, -1)
        got = swap_core(core_pick(block[1], block[0]))
        return core_pick(block[0], block[1]), got

    def gain_grad(gain, pairs):
        total = sum(jnp.sum(w.astype(F32) * g, axis=1) for w, g in pairs)
        return total / gain.astype(F32)

    def finish_units():
        live = flow.live
        classes = []
        near, far = (
            own_shard(jnp.concatenate([v[j] for j in range(CHUNKS)], axis=1))
            for v in (live.keep, live.home)
        )
        for x in range(2):
            keep, got = (x_pick(*((n, f) if x == 0 else (f, n))) for n, f in zip(near, far))
            classes += [core_pick(keep, got), core_pick(got, keep)]
        live.grad_wg, live.grad_wu = join_units(classes, groups, ff_rows, pieces, padded)
        live.ffn_gain = gain_grad(ffn_gain, ((w_gate, live.grad_wg), (w_up, live.grad_wu)))
        downs = [flow.take((DOWN, j, True))[: b - a] for j, (a, b) in enumerate(pieces)]
        live.grad_wd = jnp.concatenate(downs, axis=0)

    def finish_out():
        grad = jnp.concatenate([flow.take((OUT, n, True)) for n in range(2)], axis=1)
        flow.live.grad_wo = trade(grad)

    gain_order = [("core", 1), ("x", 1)] + group_axes()
    schedule = (
        (tables, first_norm, gather_qkv),
        (gather_out, far_low, heads),
        (attention, branch, near_low),
        (far_hidden, do(units, 0, 0)),
        (near_hidden, do(units, 0, 1), do(down_grad, 0), do(units_grad, 0)),
        (do(units, 1, 0), do(units, 1, 1), do(down_grad, 1)),
        (do(units_grad, 1), do(hidden_sum, 1)),
        (far_grad, do(hidden_sum, 0), do(down_sum, 1), do(down_sum, 0)),
        (far_result, do(home, 0), second_back, out_grad),
        (attention_back,),
        (prior_back, do(home, 1), queries_back, finish_output),
        (keys_back,),
        (first_back,),
        (finish_units, do(gain_hops, gain_order[:2])),
        (finish_out, do(gain_hops, gain_order[2:4]),),
        (do(gain_hops, gain_order[4:]),),
    )
    for work in schedule:
        flow.interval(*work)
    live = flow.live

    grads = []
    for n in range(2):
        keep, got = own_shard(flow.take((QKV, n, True)))
        grads.append((core_pick(keep, got), core_pick(got, keep)))
    grad_wq = jnp.concatenate(grads[0], axis=1)
    grad_wk = jnp.concatenate([g[:, :kv_cols] for g in grads[1]], axis=1)
    grad_wv = jnp.concatenate([g[:, kv_cols:] for g in grads[1]], axis=1)
    attn_gain_grad = gain_grad(attn_gain, zip(weights, (grad_wq, grad_wk, grad_wv)))
    return (
        live.output.reshape(1, half, width),
        live.input_grad.reshape(1, half, width),
        attn_gain_grad,
        grad_wq,
        grad_wk,
        grad_wv,
        live.head_gains[0],
        live.head_gains[1],
        live.grad_wo,
        live.ffn_gain,
        live.grad_wg,
        live.grad_wu,
        live.grad_wd,
    )


def solution(mesh):
    ny, nf = mesh.shape["seq"], mesh.shape["fsdp"]
    fine = Mesh(mesh.devices.reshape(ny, nf // 4, 2, 2), AXES)
    fsdp = ("z", "x", "core")
    rows = P(fsdp, "seq", None)
    vec, mat = P(AXES), P(AXES, None)
    in_specs = (rows, P(fsdp, None), vec, mat, mat, mat, P(), P(), mat, vec, mat, mat, mat, rows)
    out_specs = (rows, rows, vec, mat, mat, mat, P(), P(), mat, vec, mat, mat, mat)
    return jax.shard_map(body, mesh=fine, in_specs=in_specs, out_specs=out_specs, check_vma=False)
```

```python
import functools
import math

import jax
import jax.numpy as jnp
from jax import lax
from jax.experimental import pallas as pl
from jax.experimental.pallas import tpu as pltpu
from jax.sharding import Mesh, PartitionSpec as P

EPS = 1e-06
BF = jnp.bfloat16
F32 = jnp.float32
HEAD_SIZE = 64
TILE = 128
SCALE = HEAD_SIZE ** (-0.5)
VMEM_LIMIT = 56 * 2**20


def dot(a, b):
    return lax.dot_general(a, b, (((1,), (0,)), ((), ())), preferred_element_type=F32)


def dot_nt(a, b):
    return lax.dot_general(a, b, (((1,), (1,)), ((), ())), preferred_element_type=F32)


def dot_tn(a, b):
    return lax.dot_general(a, b, (((0,), (0,)), ((), ())), preferred_element_type=F32)


def call(kernel, grid, in_specs, out_specs, out_shape, name, scratch=(), scalars=()):
    scalars = [jnp.asarray(s, jnp.int32).reshape(-1) for s in scalars]
    return functools.partial(
        pl.pallas_call(
            kernel,
            grid_spec=pltpu.PrefetchScalarGridSpec(
                num_scalar_prefetch=len(scalars),
                grid=grid,
                in_specs=in_specs,
                out_specs=out_specs,
                scratch_shapes=scratch,
            ),
            out_shape=out_shape,
            compiler_params=pltpu.CompilerParams(vmem_limit_bytes=VMEM_LIMIT),
            name=name,
        ),
        *scalars,
    )


def shaped(shape, dtype):
    return jax.ShapeDtypeStruct(shape, dtype)


def whole(shape):
    return pl.BlockSpec(shape, lambda *_: (0,) * len(shape))


def once(shape):
    return pl.BlockSpec(shape, lambda *_: (0,) * len(shape), pipeline_mode=pl.Buffered(1))


def row_blocks(tile, cols):
    return pl.BlockSpec((tile, cols), lambda i, *_: (i, 0))


def group_blocks(tile, cols, group, per_group):
    return pl.BlockSpec(
        (tile, cols), lambda i, *_: (jnp.clip(i - group * per_group, 0, per_group - 1), 0)
    )


def pick_group(refs, per_group):
    value = refs[0][...]
    for g in range(1, len(refs)):
        value = jnp.where(pl.program_id(0) >= g * per_group, refs[g][...], value)
    return value


def lane_of(shape):
    return lax.broadcasted_iota(jnp.int32, shape, 1)


def half_sums(values, even):
    low = jnp.sum(jnp.where(even, values, 0.0), axis=-1, keepdims=True)
    high = jnp.sum(jnp.where(even, 0.0, values), axis=-1, keepdims=True)
    return jnp.where(even, low, high)


def turned(values, first):
    return jnp.where(first, pltpu.roll(values, TILE - 32, 1), pltpu.roll(values, 32, 1))


def project(groups, weight_all, core, q_gain, k_gain, cos, sin, q_cols, kv_cols):
    half, width = groups[0].shape
    cols = q_cols + 2 * kv_cols
    q_tiles, k_heads = q_cols // TILE, kv_cols // HEAD_SIZE
    raw_cols = (q_tiles + (k_heads + 1) // 2) * TILE
    tile = 256
    per = half // tile
    count = len(groups)
    rows = count * half

    def kernel(core_ref, *refs):
        hid, (w_ref, qg_ref, kg_ref, cos_ref, sin_ref, q_ref, kv_ref, raw_ref) = refs[:count], refs[count:]
        lane = lane_of((tile, TILE))
        even, first = lane < HEAD_SIZE, lane % HEAD_SIZE < HEAD_SIZE // 2
        out = dot(pick_group(hid, per), w_ref[...])
        cos, sin = cos_ref[...], sin_ref[...]
        raw_ref[...] = out[:, :raw_cols]
        for t in range(cols // TILE):
            x = out[:, t * TILE : (t + 1) * TILE]
            heads_left = k_heads - 2 * (t - q_tiles)
            y = x
            if heads_left > 0:
                gain = qg_ref[...] if t < q_tiles else kg_ref[...]
                y = x * lax.rsqrt(half_sums(x * x, even) * (1.0 / HEAD_SIZE) + EPS) * gain
                y = y * cos + turned(y, first) * sin
                if t >= q_tiles and heads_left == 1:
                    y = jnp.where(even, y, x)
            if t < q_tiles:
                q_ref[:, t * TILE : (t + 1) * TILE] = y.astype(BF)
            else:
                kv_ref[:, (t - q_tiles) * TILE : (t - q_tiles + 1) * TILE] = y.astype(BF)

    return call(
        kernel,
        (rows // tile,),
        [group_blocks(tile, width, g, per) for g in range(count)]
        + [pl.BlockSpec((width, cols), lambda i, c: (0, c[0]), pipeline_mode=pl.Buffered(1))]
        + [whole((1, TILE))] * 2 + [row_blocks(tile, TILE)] * 2,
        [row_blocks(tile, q_cols), row_blocks(tile, 2 * kv_cols), row_blocks(tile, raw_cols)],
        [shaped((rows, q_cols), BF), shaped((rows, 2 * kv_cols), BF), shaped((rows, raw_cols), F32)],
        "project_heads",
        scalars=[core],
    )(*groups, weight_all, q_gain, k_gain, cos, sin)


def head_grads(parts, raw, first_tile, heads, gain, cos, sin):
    rows, cols = parts[0].shape
    normed = (heads + 1) // 2
    count, tile = len(parts), 256

    def kernel(*refs):
        ds, (raw_ref, gain_ref, cos_ref, sin_ref, g_ref, sum_ref) = refs[:count], refs[count:]
        lane = lane_of((tile, TILE))
        even, first = lane < HEAD_SIZE, lane % HEAD_SIZE < HEAD_SIZE // 2
        cos, sin, gain = cos_ref[...], sin_ref[...], gain_ref[...]

        @pl.when(pl.program_id(0) == 0)
        def _():
            sum_ref[...] = jnp.zeros_like(sum_ref)

        for t in range(cols // TILE):
            at = slice(t * TILE, (t + 1) * TILE)
            d = sum(ref[:, at].astype(F32) for ref in ds)
            y = d
            if t < normed:
                x = raw_ref[:, at]
                r = lax.rsqrt(half_sums(x * x, even) * (1.0 / HEAD_SIZE) + EPS)
                n = x * r
                back = d * cos - turned(d, first) * sin
                dn = back * n
                w = back * gain
                y = r * (w - n * (half_sums(w * n, even) * (1.0 / HEAD_SIZE)))
                if heads - 2 * t == 1:
                    y = jnp.where(even, y, d)
                    dn = jnp.where(even, dn, 0.0)
                sum_ref[...] += jnp.sum(dn.reshape(tile // 8, 8, TILE), axis=0)
            g_ref[:, at] = y.astype(BF)

    raw_at = first_tile // normed
    return call(
        kernel,
        (rows // tile,),
        [row_blocks(tile, cols)] * count
        + [pl.BlockSpec((tile, normed * TILE), lambda i: (i, raw_at)), whole((1, TILE))]
        + [row_blocks(tile, TILE)] * 2,
        [row_blocks(tile, cols), whole((8, TILE))],
        [shaped((rows, cols), BF), shaped((8, TILE), F32)],
        "head_grads",
    )(*parts, raw, gain, cos, sin)


def stacked(ref, g, even):
    out = []
    for p in range(2):
        pair = ref[0, :, (2 * g + p) * TILE : (2 * g + p + 1) * TILE]
        zero = jnp.zeros_like(pair)
        out += [jnp.where(even, pair, zero), jnp.where(even, zero, pair)]
    return jnp.concatenate(out, axis=0)


def unstacked(values, p, even):
    base = 2 * p * TILE
    return jnp.where(even, values[base : base + TILE], values[base + TILE : base + 2 * TILE])


def transposed_pair(values, p, even):
    at = 2 * p * TILE
    low, high = values[:, at : at + TILE].T, values[:, at + TILE : at + 2 * TILE].T
    return jnp.where(even, low, high)


def widen(refs, heads, place):
    at = 0
    even = lane_of((TILE, TILE)) < HEAD_SIZE
    for ref in refs:
        for r in range(0, ref.shape[1], TILE):
            for t in range(heads):
                x = ref[0, r : r + TILE, t * TILE : (t + 1) * TILE].astype(F32)
                other = pltpu.roll(x, HEAD_SIZE, 1)
                for part, value in enumerate((jnp.where(even, x, other), jnp.where(even, other, x))):
                    n = 2 * t + part
                    col = slice((n % heads) * TILE, (n % heads + 1) * TILE)
                    place(n < heads, slice(at, at + TILE), col, value)
            at += TILE


def narrow(k_ref, v_ref, rows, t, heads, even):
    tiles = []
    for n in (2 * t, 2 * t + 1):
        ref = k_ref if n < heads else v_ref
        x = ref[rows, (n % heads) * TILE : (n % heads + 1) * TILE]
        tiles.append(x + pltpu.roll(x, HEAD_SIZE, 1))
    return jnp.where(even, tiles[0], tiles[1])


def key_bias(qseg_ref, kseg_ref, j, i, blocks):
    at = pl.ds(pl.multiple_of(j * TILE, TILE), TILE)
    key_at = lax.broadcasted_iota(jnp.int32, (TILE, TILE), 0) + j * TILE
    query_at = lane_of((TILE, TILE)) + (i + blocks) * TILE
    ok = (kseg_ref[0, at, :] == qseg_ref[0, pl.ds(i, 1), :]) & (key_at <= query_at)
    return at, jnp.concatenate([jnp.where(ok, 0.0, -1e30)] * 4, axis=1)


def attend(low_block, q, kv_prior, kv, qseg, kseg):
    batch, rows, cols = q.shape
    blocks = rows // TILE
    heads = kv.shape[2] // TILE
    keys = 2 * rows
    lse_rows = -(-4 * heads // 8) * 8

    def kernel(lo_ref, q_ref, prior_ref, kv_ref, qseg_ref, kseg_ref, o_ref, lse_ref, acc_ref, sum_ref, k_ref, v_ref):
        b, i = pl.program_id(0), pl.program_id(1)
        lane = lane_of((TILE, TILE))
        even = lane < HEAD_SIZE

        @pl.when(i == 0)
        def _():
            def place(is_key, at, col, value):
                (k_ref if is_key else v_ref)[at, col] = value.astype(BF)

            widen((prior_ref, kv_ref), heads, place)

        qs = [stacked(q_ref, g, even) * jnp.asarray(SCALE, BF) for g in range(heads)]
        acc_ref[...] = jnp.zeros_like(acc_ref)
        sum_ref[...] = jnp.zeros_like(sum_ref)
        seg = qseg_ref[0]
        row_at = lax.broadcasted_iota(jnp.int32, (TILE, TILE), 0) + (i + blocks) * TILE

        def step(j, carry):
            at = pl.ds(pl.multiple_of(j * TILE, TILE), TILE)
            ok = (seg == kseg_ref[0, pl.ds(j, 1), :]) & (lane + j * TILE <= row_at)
            bias = jnp.where(ok, 0.0, -1e30)
            bias = jnp.concatenate([bias] * 4, axis=0)
            for g in range(heads):
                col = slice(g * TILE, (g + 1) * TILE)
                e = jnp.exp(dot_nt(qs[g], k_ref[at, col]) + bias)
                sum_ref[g] += e
                acc_ref[g] += dot(e.astype(BF), v_ref[at, col])
            return carry

        lax.fori_loop(lo_ref[b * blocks + i], i + blocks + 1, step, 0)
        lse = jnp.zeros((TILE, TILE), F32)
        for g in range(heads):
            total = jnp.sum(sum_ref[g], axis=-1, keepdims=True)
            out = acc_ref[g] / total
            log = jnp.log(total)
            for p in range(2):
                o_ref[0, :, (2 * g + p) * TILE : (2 * g + p + 1) * TILE] = unstacked(out, p, even).astype(BF)
            for h in range(4):
                lse = jnp.where(lane == 4 * g + h, log[h * TILE : (h + 1) * TILE], lse)
        lse_ref[0, 0] = lse.T[:lse_rows]

    per_q = lambda n: pl.BlockSpec((1, TILE, n), lambda b, i, lo: (b, i, 0))
    per_b = lambda s: pl.BlockSpec((1,) + s[1:], lambda b, i, lo: (b, 0, 0))
    return call(
        kernel,
        (batch, blocks),
        [per_q(cols), per_b(kv.shape), per_b(kv.shape), per_q(1), per_b(kseg.shape)],
        [per_q(cols), pl.BlockSpec((1, 1, lse_rows, TILE), lambda b, i, lo: (b, i, 0, 0))],
        [shaped(q.shape, BF), shaped((batch, blocks, lse_rows, TILE), F32)],
        "attend",
        [pltpu.VMEM((heads, 4 * TILE, TILE), F32)] * 2 + [pltpu.VMEM((keys, heads * TILE), BF)] * 2,
        [low_block],
    )(q, kv_prior, kv, qseg, kseg)


def attend_back(low_block, q, kv_prior, kv, qseg, kseg, o, lse, do):
    batch, rows, cols = q.shape
    blocks = rows // TILE
    heads = kv.shape[2] // TILE
    keys = 2 * rows

    def kernel(lo_ref, q_ref, prior_ref, kv_ref, qseg_ref, kseg_ref, o_ref, lse_ref, do_ref, dq_ref, dprior_ref, dkv_ref, acc_ref, k_ref, kt_ref, v_ref, dk_ref, dv_ref):
        b, i = pl.program_id(0), pl.program_id(1)
        even = lane_of((TILE, TILE)) < HEAD_SIZE

        @pl.when(i == 0)
        def _():
            def place(is_key, at, col, value):
                if is_key:
                    k_ref[at, col] = value.astype(BF)
                    kt_ref[col, at] = value.T.astype(BF)
                else:
                    v_ref[at, col] = value.astype(BF)

            widen((prior_ref, kv_ref), heads, place)
            dk_ref[...] = jnp.zeros_like(dk_ref)
            dv_ref[...] = jnp.zeros_like(dv_ref)

        qs = [stacked(q_ref, g, even) * jnp.asarray(SCALE, BF) for g in range(heads)]
        dos = [stacked(do_ref, g, even) for g in range(heads)]
        lses, deltas = [], []
        for g in range(heads):
            each = []
            for p in range(2):
                at = slice((2 * g + p) * TILE, (2 * g + p + 1) * TILE)
                both = (o_ref[0, :, at].astype(F32) * do_ref[0, :, at].astype(F32)).T
                each += [
                    jnp.sum(both[n : n + HEAD_SIZE], axis=0, keepdims=True)
                    for n in (0, HEAD_SIZE)
                ]
            deltas.append(jnp.concatenate(each, axis=1))
            lses.append(
                jnp.concatenate([lse_ref[0, 0, 4 * g + h : 4 * g + h + 1, :] for h in range(4)], axis=1)
            )
        acc_ref[...] = jnp.zeros_like(acc_ref)

        def step(j, carry):
            at, bias = key_bias(qseg_ref, kseg_ref, j, i, blocks)
            for g in range(heads):
                col = slice(g * TILE, (g + 1) * TILE)
                p = jnp.exp(dot_nt(k_ref[at, col], qs[g]) + (bias - lses[g]))
                ds = (p * (dot_nt(v_ref[at, col], dos[g]) - deltas[g])).astype(BF)
                dv_ref[at, col] += dot(p.astype(BF), dos[g])
                dk_ref[at, col] += dot(ds, qs[g])
                acc_ref[g] += dot(kt_ref[col, at], ds)
            return carry

        lax.fori_loop(lo_ref[b * blocks + i], i + blocks + 1, step, 0)
        for g in range(heads):
            for p in range(2):
                dq_ref[0, :, (2 * g + p) * TILE : (2 * g + p + 1) * TILE] = (
                    transposed_pair(acc_ref[g], p, even) * SCALE
                )

        @pl.when(i == blocks - 1)
        def _():
            for r in range(0, rows, TILE):
                for t in range(heads):
                    col = slice(t * TILE, (t + 1) * TILE)
                    dprior_ref[0, r : r + TILE, col] = narrow(
                        dk_ref, dv_ref, slice(r, r + TILE), t, heads, even
                    ).astype(BF)
                    dkv_ref[0, r : r + TILE, col] = narrow(
                        dk_ref, dv_ref, slice(rows + r, rows + r + TILE), t, heads, even
                    )

    per_q = lambda n: pl.BlockSpec((1, TILE, n), lambda b, i, lo: (b, i, 0))
    per_b = lambda s: pl.BlockSpec((1,) + s[1:], lambda b, i, lo: (b, 0, 0))
    wide = (keys, heads * TILE)
    return call(
        kernel,
        (batch, blocks),
        [per_q(cols), per_b(kv.shape), per_b(kv.shape), per_b(qseg.shape), per_b(kseg.shape)]
        + [per_q(cols), pl.BlockSpec((1, 1) + lse.shape[2:], lambda b, i, lo: (b, i, 0, 0))]
        + [per_q(cols)],
        [per_q(cols), per_b(kv.shape), per_b(kv.shape)],
        [shaped(q.shape, F32), shaped(kv.shape, BF), shaped(kv.shape, F32)],
        "attend_back",
        [
            pltpu.VMEM((heads, TILE, 4 * TILE), F32),
            pltpu.VMEM(wide, BF),
            pltpu.VMEM(wide[::-1], BF),
            pltpu.VMEM(wide, BF),
            pltpu.VMEM(wide, F32),
            pltpu.VMEM(wide, F32),
        ],
        [low_block],
    )(q, kv_prior, kv, qseg, kseg, o, lse, do)


def hidden_units(hidden, low, gate_up, down):
    half, width = hidden[0].shape
    cols = down.shape[0]
    tile = 256
    per = half // tile
    count = len(hidden)

    def kernel(*refs):
        hid, lows = refs[:count], refs[count : 2 * count]
        gu_ref, wd_ref, act_ref, grad_ref = refs[2 * count :]
        x, y = pick_group(hid, per), pick_group(lows, per)
        step = 256
        for c in range(0, cols, step):
            n = min(step, cols - c)
            gate = dot(x, gu_ref[:, c : c + n])
            up = dot(x, gu_ref[:, cols + c : cols + c + n])
            grad = dot_nt(y, wd_ref[c : c + n, :])
            sig = 1.0 / (1.0 + jnp.exp(-gate))
            silu = gate * sig
            act_ref[:, c : c + n] = (silu * up).astype(BF)
            grad_ref[:, c : c + n] = (grad * up * (sig * (1.0 + gate * (1.0 - sig)))).astype(BF)
            grad_ref[:, cols + c : cols + c + n] = (grad * silu).astype(BF)

    groups = [group_blocks(tile, width, g, per) for g in range(count)]
    rows = count * half
    return call(
        kernel,
        (rows // tile,),
        groups + groups + [once(gate_up.shape), once(down.shape)],
        [row_blocks(tile, cols), row_blocks(tile, 2 * cols)],
        [shaped((rows, cols), BF), shaped((rows, 2 * cols), BF)],
        "hidden_units",
    )(*hidden, *low, gate_up, down)


def tall_grad(groups, rights, bit, name):
    half, width = groups[0].shape
    cols = rights[0].shape[1]
    count, pairs = len(groups), len(rights)
    tile = 512
    steps = width // tile
    split = bit is not None
    side = steps // 2 if split else 0

    def kernel(bit_ref, *refs):
        lefts, right, outs = refs[:count], refs[count : count + pairs], refs[count + pairs :]
        total = None
        for g in range(count):
            r = right[g // 2][(g % 2) * half : (g % 2 + 1) * half, :]
            term = dot_tn(lefts[g][...], r)
            total = term if total is None else total + term

        @pl.when(pl.program_id(0) >= side)
        def _():
            outs[0][...] = total.astype(BF)

        if split:

            @pl.when(pl.program_id(0) < side)
            def _():
                outs[1][...] = total.astype(BF)

    def column(i, bit):
        if not split:
            return (0, i)
        return (0, i % side + side * jnp.where(i >= side, bit[0], 1 - bit[0]))

    out_specs = [pl.BlockSpec((tile, cols), lambda i, b: (jnp.maximum(i - side, 0), 0))]
    if split:
        out_specs.append(pl.BlockSpec((tile, cols), lambda i, b: (jnp.minimum(i, side - 1), 0)))
    return call(
        kernel,
        (steps,),
        [pl.BlockSpec((half, tile), column)] * count + [once(r.shape) for r in rights],
        out_specs,
        [shaped(((steps - side) * tile, cols), BF)] * len(out_specs),
        name,
        scalars=[bit if split else 0],
    )(*groups, *rights)


def wide_grad(lefts, groups, name):
    half, width = groups[0].shape
    cols = lefts[0].shape[1]
    count, pairs = len(groups), len(lefts)
    tile = 512

    def kernel(*refs):
        total = None
        for g in range(count):
            left = refs[g // 2][(g % 2) * half : (g % 2 + 1) * half, :]
            term = dot_tn(left, refs[pairs + g][...])
            total = term if total is None else total + term
        refs[-1][...] = total.astype(BF)

    return call(
        kernel,
        (width // tile,),
        [once(a.shape) for a in lefts] + [pl.BlockSpec((half, tile), lambda i: (0, i))] * count,
        pl.BlockSpec((cols, tile), lambda i: (0, i)),
        shaped((cols, width), BF),
        name,
    )(*lefts, *groups)


def sum_products(lefts, rights, transposed, name, core=0, part=None):
    rows = lefts[0].shape[0]
    width = rights[0].shape[0] if transposed else rights[0].shape[1]
    tile, count = 512, len(lefts)

    def kernel(core_ref, *refs):
        total = None
        for a, b in zip(refs[:count], refs[count : 2 * count]):
            term = dot_nt(a[...], b[...]) if transposed else dot(a[...], b[...])
            total = term if total is None else total + term
        refs[-2][...] = total[: rows // 2]
        refs[-1][...] = total[rows // 2 :].astype(BF)

    at = lambda c: c[0] if part else 0
    if transposed:
        right = [
            pl.BlockSpec((tile, part or r.shape[1]), lambda i, c: (i, at(c))) for r in rights
        ]
    else:
        right = [
            pl.BlockSpec((part or r.shape[0], tile), lambda i, c: (at(c), i)) for r in rights
        ]
    column = pl.BlockSpec((rows // 2, tile), lambda i, c: (0, i))
    return call(
        kernel,
        (width // tile,),
        [once(a.shape) for a in lefts] + right,
        [column, column],
        [shaped((rows // 2, width), F32), shaped((rows // 2, width), BF)],
        name,
        scalars=[core],
    )(*lefts, *rights)


def first_sum(grad_q, grad_kv, weights, core):
    rows, part = grad_kv.shape
    width, tile = weights.shape[0], 512
    count = grad_q.shape[1] // part + 1

    def kernel(core_ref, *refs):
        total = None
        for a, b in zip(refs[:count], refs[count : 2 * count]):
            term = dot_nt(a[...], b[...])
            total = term if total is None else total + term
        refs[-2][...] = total[: rows // 2]
        refs[-1][...] = total[rows // 2 :].astype(BF)

    column_of = lambda n: pl.BlockSpec(
        (rows, part), lambda i, c: (0, n), pipeline_mode=pl.Buffered(1)
    )
    weight_of = lambda n: pl.BlockSpec((tile, part), lambda i, c: (i, count * c[0] + n))
    column = pl.BlockSpec((rows // 2, tile), lambda i, c: (0, i))
    return call(
        kernel,
        (width // tile,),
        [column_of(n) for n in range(count - 1)] + [column_of(0)]
        + [weight_of(n) for n in range(count)],
        [column, column],
        [shaped((rows // 2, width), F32), shaped((rows // 2, width), BF)],
        "first_sum",
        scalars=[core],
    )(*[grad_q] * (count - 1), grad_kv, *[weights] * count)


def token_product(groups, weight, core, part, name):
    half, width = groups[0].shape
    tile = 256
    per, count = half // tile, len(groups)

    def kernel(core_ref, *refs):
        refs[-1][...] = dot_nt(pick_group(refs[:count], per), refs[count][...]).astype(BF)

    return call(
        kernel,
        (count * per,),
        [group_blocks(tile, width, g, per) for g in range(count)]
        + [pl.BlockSpec((part, width), lambda i, c: (c[0], 0), pipeline_mode=pl.Buffered(1))],
        row_blocks(tile, part),
        shaped((count * half, part), BF),
        name,
        scalars=[core],
    )(*groups, weight)


def unit_moves(groups, size, pieces, padded):
    moves = []
    for n in range(2):
        for j, (a, b) in enumerate(pieces):
            for owner in range(4 * groups):
                at = ((2 * j + n) * groups + owner // 4) * padded
                moves.append((n, owner % 4, owner * size + a, at, b - a))
    return moves


def split_units(gate, up, groups, size, pieces, padded):
    rows, cols = gate.shape
    moves = unit_moves(groups, size, pieces, padded)
    share = 2 * len(pieces) * groups * padded

    def kernel(gate_ref, up_ref, out_ref, wide, kinds):
        kinds[...] = jnp.zeros_like(kinds)
        for n, ref in enumerate((gate_ref, up_ref)):
            wide[...] = ref[...].astype(F32)
            for m, c, src, dst, width in moves:
                if m == n:
                    kinds[c, :, dst : dst + width] = wide[:, src : src + width]
        out_ref[...] = kinds[...].astype(BF)

    out = shaped((4, rows, share), BF)
    return call(
        kernel,
        (1,),
        [whole((rows, cols))] * 2,
        whole(out.shape),
        out,
        "split_units",
        [pltpu.VMEM((rows, cols), F32), pltpu.VMEM(out.shape, F32)],
    )(gate, up)


def join_units(classes, groups, size, pieces, padded):
    rows = classes[0].shape[0]
    moves = unit_moves(groups, size, pieces, padded)

    def kernel(a_ref, b_ref, c_ref, d_ref, gate_ref, up_ref):
        for n, c, src, dst, width in moves:
            ref = (a_ref, b_ref, c_ref, d_ref)[c]
            (gate_ref, up_ref)[n][:, src : src + width] = ref[:, dst : dst + width]

    out = shaped((rows, 4 * groups * size), F32)
    return call(
        kernel,
        (1,),
        [whole(classes[0].shape)] * 4,
        [whole(out.shape)] * 2,
        [out] * 2,
        "join_units",
    )(*classes)


QUERY_HEADS = 24
KEY_VALUE_HEADS = 6
AXES = ("seq", "z", "x", "core")
CHUNKS = 2
UNITS, DOWN, OUT, QKV = range(4)
PLAN = {
    (UNITS, 0): (0, 2, 3),
    (DOWN, 0): (0, 2, 3),
    (UNITS, 1): (3, 5, 6),
    (DOWN, 1): (3, 5, 6),
    (DOWN, 0, True): (7, 10, 12),
    (UNITS, 0, True): (7, 8, 10),
    (DOWN, 1, True): (8, 10, 12),
    (UNITS, 1, True): (8, 10, 13),
    (OUT, 0, True): (13, 14, 15, 16),
    (OUT, 1, True): (14, 15, 16, 17),
    (QKV, 0, True): (15, 16, 17, 18),
    (QKV, 1, True): (16, 17, 18, 19),
}


def swap_core(value):
    return lax.ppermute(value, "core", [(0, 1), (1, 0)])


def core_pick(first, second):
    return jnp.where(lax.axis_index("core") == 0, first, second)


def core_concat(own, other, axis=0):
    return core_pick(
        jnp.concatenate([own, other], axis=axis), jnp.concatenate([other, own], axis=axis)
    )


def swap_seq(value):
    return lax.ppermute(value, "seq", [(0, 1), (1, 0)])


def swap_x(value):
    return lax.ppermute(value, "x", [(0, 1), (1, 0)])


def x_pick(first, second):
    return jnp.where(lax.axis_index("x") == 0, first, second)


def group_axes():
    bits = lax.axis_size("z").bit_length() - 1
    return [("seq", 1)] + [("z", 1 << k) for k in reversed(range(bits))]


def orders_of(name):
    cube = group_axes()
    far, near, seq = cube[1:-1], cube[-1:], cube[:1]
    what, number = name[:2]
    if what in (OUT, QKV):
        x = [("x", 1)]
        cube = cube + x
        stages = [far, seq, near, x] if number else [far, x, near, seq]
    else:
        stages = [far, seq, near] if what == DOWN else [far, near, seq]
    return cube, [s[::-1] for s in stages[::-1]] if len(name) > 2 else stages


def hop_bit(hop):
    axis, step = hop
    return lax.axis_index(axis) // step % 2


def exchange(value, hop):
    axis, step = hop
    return lax.ppermute(value, axis, [(i, i ^ step) for i in range(lax.axis_size(axis))])


def place_kernel(bit_ref, own_ref, got_ref, out_ref):
    bit = bit_ref[0]
    out_ref[:, pl.ds(bit, 1)] = own_ref[...][:, None]
    out_ref[:, pl.ds(1 - bit, 1)] = got_ref[...][:, None]


def placed(own, got, dim, bit):
    shape = own.shape
    lead, inner = math.prod(shape[:dim]), math.prod(shape[dim:-2])
    flat = (lead, inner) + shape[-2:]
    part = math.gcd(inner, 2) if lead == 1 else inner
    block = (1, part) + shape[-2:]
    side = pl.BlockSpec(block, lambda i, j, bit: (i, j, 0, 0))
    out = call(
        place_kernel,
        (lead, inner // part),
        [side, side],
        pl.BlockSpec((1, 2) + block[1:], lambda i, j, bit: (i, 0, j, 0, 0)),
        shaped((lead, 2) + flat[1:], own.dtype),
        "place",
        scalars=[bit],
    )(own.reshape(flat), got.reshape(flat))
    return out.reshape(shape[:dim] + (2,) + shape[dim + 1 :])


class Values:
    def __init__(self):
        for name in ("low", "hidden", "wgu", "wd", "act", "ggu", "keep", "home", "hidden_sum", "down_sum"):
            setattr(self, name, {})


class Flow:
    def __init__(self):
        self.live = Values()
        self.rest, self.flight, self.later, self.stage, self.now = {}, {}, {}, {}, 0

    def fence(self):
        values, parts = lax.optimization_barrier((vars(self.live), self.rest))
        vars(self.live).update(values)
        self.rest = parts

    def gather(self, name, block):
        self.rest[name] = block.reshape((1,) * len(orders_of(name)[0]) + block.shape)
        self.stage[name] = 0

    def scatter(self, name, rows, grad, sent=None):
        self.stage[name] = 0
        shape = [2] * len(orders_of(name)[0])
        if sent is None:
            self.rest[name] = grad.reshape(shape + [rows, grad.shape[1]])
        else:
            shape[self.hop(name)[1]] = 1
            self.rest[name] = tuple(v.reshape(shape + [rows, v.shape[1]]) for v in (grad, sent))

    def hop(self, name):
        cube, stages = orders_of(name)
        hop = sum(stages, [])[self.stage[name]]
        return hop, cube.index(hop)

    def start(self, name):
        hop, dim = self.hop(name)
        bit, value = hop_bit(hop), self.rest.pop(name)
        if isinstance(value, tuple):
            value, sent = value
        elif len(name) > 2:
            sent = lax.dynamic_slice_in_dim(value, 1 - bit, 1, dim)
        else:
            sent = value
        self.flight[name] = (value, exchange(sent, hop), dim, bit)

    def land(self, name):
        keep, got, dim, bit = self.flight.pop(name)
        self.stage[name] += 1
        stages = orders_of(name)[1]
        ends = [sum(map(len, stages[: k + 1])) for k in range(len(stages))]
        last = self.stage[name] == ends[-1]
        if len(name) > 2:
            if keep.shape[dim] == 2:
                keep = lax.dynamic_slice_in_dim(keep, bit, 1, dim)
            total = keep.astype(F32) + got.astype(F32)
            self.rest[name] = total if last else total.astype(BF)
        elif last:
            self.rest[name] = (keep, got)
            self.stage[name] = (dim, bit)
        else:
            self.rest[name] = placed(keep, got, dim, bit)
        if not last and self.stage[name] not in ends:
            self.start(name)
            self.land(name)

    def take(self, name):
        value = self.rest.pop(name)
        dims = len(orders_of(name)[0])
        if len(name) > 2:
            return value.reshape(value.shape[dims:])
        value = placed(*value, *self.stage[name])
        return value.reshape((-1,) + value.shape[dims + 1 :])

    def post(self, value, name, key=None, wait=0):
        self.later[name, key] = (value, self.now + wait)

    def interval(self, *work):
        active = [name for name, at in PLAN.items() if self.now in at]
        for name in active:
            self.start(name)
        for piece in work:
            piece()
        for name in active:
            self.land(name)
        for name, key in [n for n, (_, at) in self.later.items() if at == self.now]:
            value = self.later.pop((name, key))[0]
            if key is None:
                setattr(self.live, name, value)
            else:
                getattr(self.live, name)[key] = value
        self.fence()
        self.now += 1


def row_norm(values):
    scale = lax.rsqrt(jnp.mean(values * values, axis=-1, keepdims=True) + EPS)
    return values * scale, scale


def norm_back(grad, normed, scale, gain):
    u = grad * gain
    return scale * (u - normed * jnp.mean(u * normed, axis=-1, keepdims=True))


def doc_positions(segment_row):
    length = segment_row.shape[-1]
    places = jnp.arange(length, dtype=jnp.int32)
    earlier = jnp.concatenate([segment_row[..., :1] + 1, segment_row[..., :-1]], axis=-1)
    starts = jnp.where(segment_row != earlier, places, 0)
    latest = jnp.max(
        jnp.where(places[None, :] <= places[:, None], starts[..., None, :], 0), axis=-1
    )
    return places - latest


def rotary_tables(positions):
    pair_count = HEAD_SIZE // 2
    frequencies = jnp.exp(
        jnp.arange(pair_count, dtype=F32) * (-2.0 * math.log(10000.0) / HEAD_SIZE)
    )
    phases = positions.astype(F32)[..., None] * frequencies
    cos, sin = jnp.cos(phases), jnp.sin(phases)
    return jnp.tile(cos, (1, 4)), jnp.tile(jnp.concatenate([-sin, sin], axis=1), (1, 2))


def split_rows(rows, pieces):
    units, rest = rows // 8, rows % 8
    sizes = [8 * (units // pieces + (i < units % pieces)) for i in range(pieces)]
    sizes[-1] += rest
    ends = [sum(sizes[: i + 1]) for i in range(pieces)]
    return [(e - s, e) for s, e in zip(sizes, ends)]


def halves(w):
    n = w.shape[1] // 2
    return w[:, :n], w[:, n:]


def body(
    tokens,
    segments,
    attn_gain,
    w_query,
    key_projection_weight,
    value_projection_weight,
    query_norm_gain,
    key_gain,
    w_out,
    ffn_gain,
    w_gate,
    w_up,
    w_down,
    cotangent,
):
    _, half, width = tokens.shape
    ny, nz, nx = (lax.axis_size(a) for a in ("seq", "z", "x"))
    groups = ny * nz
    core, seq, x_at = (lax.axis_index(a) for a in ("core", "seq", "x"))
    q_cols, kv_cols = w_query.shape[1] // 2, key_projection_weight.shape[1] // 2
    kv_heads = KEY_VALUE_HEADS // 2
    out_rows, ff_rows, in_rows = w_out.shape[0], w_down.shape[0], w_gate.shape[0]
    pieces = split_rows(ff_rows, CHUNKS)
    step = TILE // math.gcd(TILE, groups)
    padded = -(-max(b - a for a, b in pieces) // step) * step
    share = groups * padded
    flow = Flow()
    do = lambda f, *a: (lambda: f(*a))

    def pair(value):
        return [value, swap_core(value)]

    def trade(value):
        return lax.ppermute(value, ("seq", "core"), [(0, 0), (1, 2), (2, 1), (3, 3)])

    weights = (w_query, key_projection_weight, value_projection_weight)
    lows, highs = zip(*(halves(w) for w in weights))
    gains = jnp.pad(jnp.stack([attn_gain, ffn_gain], axis=1), ((0, 0), (0, TILE - 2)))
    block = jnp.concatenate(lows + highs + (gains,), axis=1)
    block = jnp.concatenate(
        [block, jnp.pad(w_out, ((0, 0), (0, block.shape[1] - width)))], axis=0
    )
    gathered = lax.all_gather(block, AXES, axis=0)

    quarters = split_units(w_gate, w_up, groups, ff_rows, pieces, padded)
    mine = [core_pick(quarters[2 * x], quarters[2 * x + 1]) for x in range(2)]
    theirs = [core_pick(quarters[2 * x + 1], quarters[2 * x]) for x in range(2)]
    sent = x_pick(jnp.concatenate(theirs), jnp.concatenate(theirs[::-1]))
    got = swap_core(sent)
    near = core_concat(x_pick(mine[0], mine[1]), got[:in_rows])
    far = swap_x(core_concat(x_pick(mine[1], mine[0]), got[in_rows:]))
    block = x_pick(jnp.concatenate([near, far]), jnp.concatenate([far, near]))
    live = flow.live
    for j, (a, b) in enumerate(pieces):
        units_block = block[:, 2 * j * share : 2 * (j + 1) * share]
        down_block = jnp.pad(w_down[a:b], ((0, padded - b + a), (0, 0)))
        flow.gather((UNITS, j), units_block)
        flow.gather((DOWN, j), down_block)

    def take_gathered():
        live = flow.live
        live.qkv = gathered[:, :in_rows].reshape(width, -1)
        live.out = gathered[:, in_rows:, :width].reshape(-1, width)

    def tables():
        live = flow.live
        segments_pair = jnp.concatenate(pair(segments), axis=0)
        positions = doc_positions(segments_pair)
        own_start = seq * half
        own_positions = lax.dynamic_slice_in_dim(positions, own_start, half, 1)
        order_ids = jnp.where(segments_pair < 0, 1 << 20, segments_pair)
        own_ids = lax.dynamic_slice_in_dim(order_ids, own_start, half, 1)
        prior_ids = lax.dynamic_slice_in_dim(order_ids, jnp.maximum(own_start - half, 0), half, 1)
        prior_ids = jnp.where(own_start >= half, prior_ids, -2)
        key_ids = jnp.concatenate([prior_ids, own_ids], axis=1)
        low_block = jnp.sum(key_ids[:, None, :] < own_ids[:, ::TILE, None], axis=-1) // TILE
        live.low_block = low_block.astype(jnp.int32)
        live.query_rows, live.query_columns = own_ids.reshape(2, -1, TILE), own_ids[:, :, None]
        live.key_rows, live.key_columns = key_ids.reshape(2, -1, TILE), key_ids[:, :, None]
        live.cos, live.sin = rotary_tables(own_positions.reshape(2 * half))
        live.q_gain = jnp.tile(query_norm_gain.astype(F32), 2).reshape(1, TILE)
        live.k_gain = jnp.tile(key_gain.astype(F32), 2).reshape(1, TILE)

    def first_norm():
        live = flow.live
        live.low[0] = pair(cotangent.reshape(half, width))
        live.normed, live.scale = row_norm(tokens.reshape(half, width).astype(F32))

    def far_low():
        flow.post(swap_x(flow.live.low[0][0]), "far_low")

    def near_low():
        flow.live.low[1] = pair(flow.live.far_low)

    def first_hidden():
        live = flow.live
        n = q_cols + 2 * kv_cols
        live.gains = live.qkv[:, 2 * n : 2 * n + 2].T.astype(F32)
        live.hidden_first = pair((live.normed * live.gains[0]).astype(BF))

    def heads():
        live = flow.live
        q_rot, kv, live.raw = project(
            live.hidden_first, live.qkv, core, live.q_gain, live.k_gain, live.cos,
            live.sin, q_cols, kv_cols,
        )
        live.q, live.kv = q_rot.reshape(2, half, -1), kv.reshape(2, half, -1)

    def prior_keys():
        flow.post(swap_seq(flow.live.kv), "prior_kv")

    def attention():
        live = flow.live
        attn, live.lse = attend(
            live.low_block, live.q, live.prior_kv, live.kv, live.query_columns, live.key_rows
        )
        live.attn = attn.reshape(2 * half, q_cols)

    def near_rows(sums):
        return sums[0] + swap_core(sums[1]).astype(F32)

    def branch_sum():
        live = flow.live
        live.branch = sum_products([live.attn], [live.out], False, "branch", core, q_cols)

    def branch():
        live = flow.live
        live.middle = tokens.reshape(half, width).astype(F32) + near_rows(live.branch)
        live.normed2, live.scale2 = row_norm(live.middle)
        live.hidden[0] = pair((live.normed2 * live.gains[1]).astype(BF))

    def far_hidden():
        flow.post(swap_x(flow.live.hidden[0][0]), "far_hidden")

    def near_hidden():
        flow.live.hidden[1] = pair(flow.live.far_hidden)

    def units(j, h):
        live = flow.live
        if h == 0:
            live.wgu[j], live.wd[j] = flow.take((UNITS, j)), flow.take((DOWN, j))
        live.act[j, h], live.ggu[j, h] = hidden_units(
            live.hidden[h], live.low[h], live.wgu[j], live.wd[j]
        )

    def down_grad(j):
        live = flow.live
        acts = [live.act[j, h] for h in range(2)]
        grad = wide_grad(acts, live.low[0] + live.low[1], "down_grad")
        flow.scatter((DOWN, j, True), padded, grad)

    def units_grad(j):
        live = flow.live
        grads = [live.ggu[j, h] for h in range(2)]
        grads = tall_grad(live.hidden[0] + live.hidden[1], grads, seq, "units_grad")
        flow.scatter((UNITS, j, True), 4 * in_rows, *grads)

    def hidden_sum(h):
        live = flow.live
        js = range(CHUNKS)
        live.hidden_sum[h] = sum_products(
            [live.ggu[j, h] for j in js], [live.wgu[j] for j in js], True, "hidden_sum"
        )

    def near_hidden_sums():
        live = flow.live
        live.far_grad_sum = near_rows(live.hidden_sum.pop(1)).astype(BF)
        live.near_grad = near_rows(live.hidden_sum.pop(0))

    def far_grad():
        flow.post(swap_x(flow.live.far_grad_sum), "far_grad")

    def down_sum(h):
        live = flow.live
        js = range(CHUNKS)
        live.down_sum[h] = sum_products(
            [live.act[j, h] for j in js], [live.wd[j] for j in js], False, "down_sum"
        )

    def near_down_sums():
        live = flow.live
        live.far_result_sum = near_rows(live.down_sum.pop(1)).astype(BF)
        live.near_result = near_rows(live.down_sum.pop(0))

    def far_result():
        flow.post(swap_x(flow.live.far_result_sum), "far_result")

    def second_back():
        live = flow.live
        grad = live.near_grad + live.far_grad.astype(F32)
        live.grad_middle = cotangent.reshape(half, width).astype(F32) + norm_back(
            grad, live.normed2, live.scale2, live.gains[1]
        )
        live.grad_branch = pair(live.grad_middle.astype(BF))

    def out_grad():
        live = flow.live
        live.grad_attn = token_product(
            live.grad_branch, live.out, core, q_cols, "grad_attn"
        )
        grad = wide_grad([live.attn], live.grad_branch, "out_grad")
        grad = grad.reshape(nz * nx, 2, out_rows, width).transpose(1, 0, 2, 3)
        grad = grad.reshape(groups * nx * out_rows, width)
        flow.scatter((OUT, 0, True), out_rows, grad[:, : width // 2])
        flow.scatter((OUT, 1, True), out_rows, grad[:, width // 2 :])

    def attention_back():
        live = flow.live
        dq, live.sent_dkv, live.dkv = attend_back(
            live.low_block, live.q, live.prior_kv, live.kv, live.query_rows,
            live.key_columns, live.attn.reshape(2, half, q_cols), live.lse,
            live.grad_attn.reshape(2, half, q_cols),
        )
        live.dq = dq.reshape(2 * half, q_cols)

    def prior_back():
        flow.post(swap_seq(flow.live.sent_dkv), "prior_dkv")

    def queries_back():
        live = flow.live
        live.grad_q, live.q_part = head_grads(
            [live.dq], live.raw, 0, q_cols // HEAD_SIZE, live.q_gain, live.cos, live.sin
        )
        grads = tall_grad(live.hidden_first, [live.grad_q], seq, "q_grad")
        flow.scatter((QKV, 0, True), 2 * in_rows, *grads)

    def keys_back():
        live = flow.live
        tall = lambda v: v.reshape(2 * half, -1)
        live.grad_kv, k_part = head_grads(
            [tall(live.dkv), tall(live.prior_dkv)], live.raw, q_cols // TILE,
            kv_cols // HEAD_SIZE, live.k_gain, live.cos, live.sin,
        )
        grad = tall_grad(live.hidden_first, [live.grad_kv], None, "kv_grad")
        flow.scatter((QKV, 1, True), 2 * in_rows, grad[0])
        parts = jnp.stack([live.q_part, k_part]).sum(axis=1)
        live.head_gains = parts.reshape(2, 2, HEAD_SIZE).sum(axis=1)

    def first_sums():
        live = flow.live
        live.first = first_sum(live.grad_q, live.grad_kv, live.qkv, core)

    def first_back():
        live = flow.live
        live.input_grad = live.grad_middle + norm_back(
            near_rows(live.first), live.normed, live.scale, live.gains[0]
        )

    def finish_output():
        live = flow.live
        total = live.near_result + live.far_result.astype(F32)
        live.output = (live.middle + total).astype(BF)

    def gain_hops(hops):
        for hop in hops:
            flow.live.head_gains = flow.live.head_gains + exchange(flow.live.head_gains, hop)

    def home(j):
        rows = flow.take((UNITS, j, True)).reshape(2, 2 * in_rows, -1)
        flow.live.keep[j] = x_pick(rows[0], rows[1])
        flow.post(swap_x(x_pick(rows[1], rows[0])), "home", j)

    def own_shard(block):
        block = block.reshape(2, in_rows, -1)
        got = swap_core(core_pick(block[1], block[0]))
        return core_pick(block[0], block[1]), got

    def gain_grad(gain, pairs):
        total = sum(jnp.sum(w.astype(F32) * g, axis=1) for w, g in pairs)
        return total / gain.astype(F32)

    def finish_units():
        live = flow.live
        classes = []
        near, far = (
            own_shard(jnp.concatenate([v[j] for j in range(CHUNKS)], axis=1))
            for v in (live.keep, live.home)
        )
        for x in range(2):
            keep, got = (x_pick(*((n, f) if x == 0 else (f, n))) for n, f in zip(near, far))
            classes += [core_pick(keep, got), core_pick(got, keep)]
        live.grad_wg, live.grad_wu = join_units(classes, groups, ff_rows, pieces, padded)
        live.ffn_gain = gain_grad(ffn_gain, ((w_gate, live.grad_wg), (w_up, live.grad_wu)))
        downs = [flow.take((DOWN, j, True))[: b - a] for j, (a, b) in enumerate(pieces)]
        live.grad_wd = jnp.concatenate(downs, axis=0)

    def finish_out():
        grad = jnp.concatenate([flow.take((OUT, n, True)) for n in range(2)], axis=1)
        flow.live.grad_wo = trade(grad)

    gain_order = [("core", 1), ("x", 1)] + group_axes()
    schedule = (
        (tables, first_norm, take_gathered),
        (first_hidden,),
        (heads, prior_keys),
        (far_low, attention, branch_sum),
        (branch, near_low),
        (far_hidden, do(units, 0, 0)),
        (near_hidden, do(units, 0, 1), do(down_grad, 0), do(units_grad, 0)),
        (do(units, 1, 0), do(units, 1, 1), do(down_grad, 1), do(units_grad, 1)),
        (do(hidden_sum, 1), do(hidden_sum, 0)),
        (near_hidden_sums,),
        (far_grad, do(down_sum, 1), do(down_sum, 0)),
        (second_back, near_down_sums),
        (do(home, 0), out_grad),
        (far_result, attention_back),
        (prior_back, do(home, 1), queries_back),
        (keys_back,),
        (first_sums,),
        (first_back, finish_output, do(gain_hops, gain_order[:2])),
        (finish_units, finish_out, do(gain_hops, gain_order[2:4])),
        (do(gain_hops, gain_order[4:]),),
    )
    for work in schedule:
        flow.interval(*work)
    live = flow.live

    grads = []
    for n in range(2):
        keep, got = own_shard(flow.take((QKV, n, True)))
        grads.append((core_pick(keep, got), core_pick(got, keep)))
    grad_wq = jnp.concatenate(grads[0], axis=1)
    grad_wk = jnp.concatenate([g[:, :kv_cols] for g in grads[1]], axis=1)
    grad_wv = jnp.concatenate([g[:, kv_cols:] for g in grads[1]], axis=1)
    attn_gain_grad = gain_grad(attn_gain, zip(weights, (grad_wq, grad_wk, grad_wv)))
    return (
        live.output.reshape(1, half, width),
        live.input_grad.reshape(1, half, width),
        attn_gain_grad,
        grad_wq,
        grad_wk,
        grad_wv,
        live.head_gains[0],
        live.head_gains[1],
        live.grad_wo,
        live.ffn_gain,
        live.grad_wg,
        live.grad_wu,
        live.grad_wd,
    )


def solution(mesh):
    ny, nf = mesh.shape["seq"], mesh.shape["fsdp"]
    fine = Mesh(mesh.devices.reshape(ny, nf // 4, 2, 2), AXES)
    fsdp = ("z", "x", "core")
    rows = P(fsdp, "seq", None)
    vec, mat = P(AXES), P(AXES, None)
    in_specs = (rows, P(fsdp, None), vec, mat, mat, mat, P(), P(), mat, vec, mat, mat, mat, rows)
    out_specs = (rows, rows, vec, mat, mat, mat, P(), P(), mat, vec, mat, mat, mat)
    return jax.shard_map(body, mesh=fine, in_specs=in_specs, out_specs=out_specs, check_vma=False)
```

```python
import functools
import math

import jax
import jax.numpy as jnp
from jax import lax
from jax.experimental import pallas as pl
from jax.experimental.pallas import tpu as pltpu
from jax.sharding import Mesh, PartitionSpec as P

EPS = 1e-06
BF = jnp.bfloat16
F32 = jnp.float32
HEAD_SIZE = 64
TILE = 128
SCALE = HEAD_SIZE ** (-0.5)
VMEM_LIMIT = 56 * 2**20


def dot(a, b):
    return lax.dot_general(a, b, (((1,), (0,)), ((), ())), preferred_element_type=F32)


def dot_nt(a, b):
    return lax.dot_general(a, b, (((1,), (1,)), ((), ())), preferred_element_type=F32)


def dot_tn(a, b):
    return lax.dot_general(a, b, (((0,), (0,)), ((), ())), preferred_element_type=F32)


def call(kernel, grid, in_specs, out_specs, out_shape, name, scratch=(), scalars=()):
    scalars = [jnp.asarray(s, jnp.int32).reshape(-1) for s in scalars]
    return functools.partial(
        pl.pallas_call(
            kernel,
            grid_spec=pltpu.PrefetchScalarGridSpec(
                num_scalar_prefetch=len(scalars),
                grid=grid,
                in_specs=in_specs,
                out_specs=out_specs,
                scratch_shapes=scratch,
            ),
            out_shape=out_shape,
            compiler_params=pltpu.CompilerParams(vmem_limit_bytes=VMEM_LIMIT),
            name=name,
        ),
        *scalars,
    )


def shaped(shape, dtype):
    return jax.ShapeDtypeStruct(shape, dtype)


def whole(shape):
    return pl.BlockSpec(shape, lambda *_: (0,) * len(shape))


def once(shape):
    return pl.BlockSpec(shape, lambda *_: (0,) * len(shape), pipeline_mode=pl.Buffered(1))


def row_blocks(tile, cols):
    return pl.BlockSpec((tile, cols), lambda i, *_: (i, 0))


def group_blocks(tile, cols, group, per_group):
    return pl.BlockSpec(
        (tile, cols), lambda i, *_: (jnp.clip(i - group * per_group, 0, per_group - 1), 0)
    )


def pick_group(refs, per_group):
    value = refs[0][...]
    for g in range(1, len(refs)):
        value = jnp.where(pl.program_id(0) >= g * per_group, refs[g][...], value)
    return value


def lane_of(shape):
    return lax.broadcasted_iota(jnp.int32, shape, 1)


def half_sums(values, even):
    low = jnp.sum(jnp.where(even, values, 0.0), axis=-1, keepdims=True)
    high = jnp.sum(jnp.where(even, 0.0, values), axis=-1, keepdims=True)
    return jnp.where(even, low, high)


def turned(values, first):
    return jnp.where(first, pltpu.roll(values, TILE - 32, 1), pltpu.roll(values, 32, 1))


def project(groups, weight_all, core, q_gain, k_gain, cos, sin, q_cols, kv_cols):
    half, width = groups[0].shape
    cols = q_cols + 2 * kv_cols
    q_tiles, k_heads = q_cols // TILE, kv_cols // HEAD_SIZE
    raw_cols = (q_tiles + (k_heads + 1) // 2) * TILE
    tile = 256
    per = half // tile
    count = len(groups)
    rows = count * half

    def kernel(core_ref, *refs):
        hid, (w_ref, qg_ref, kg_ref, cos_ref, sin_ref, q_ref, kv_ref, raw_ref) = refs[:count], refs[count:]
        lane = lane_of((tile, TILE))
        even, first = lane < HEAD_SIZE, lane % HEAD_SIZE < HEAD_SIZE // 2
        out = dot(pick_group(hid, per), w_ref[...])
        cos, sin = cos_ref[...], sin_ref[...]
        raw_ref[...] = out[:, :raw_cols]
        for t in range(cols // TILE):
            x = out[:, t * TILE : (t + 1) * TILE]
            heads_left = k_heads - 2 * (t - q_tiles)
            y = x
            if heads_left > 0:
                gain = qg_ref[...] if t < q_tiles else kg_ref[...]
                y = x * lax.rsqrt(half_sums(x * x, even) * (1.0 / HEAD_SIZE) + EPS) * gain
                y = y * cos + turned(y, first) * sin
                if t >= q_tiles and heads_left == 1:
                    y = jnp.where(even, y, x)
            if t < q_tiles:
                q_ref[:, t * TILE : (t + 1) * TILE] = y.astype(BF)
            else:
                kv_ref[:, (t - q_tiles) * TILE : (t - q_tiles + 1) * TILE] = y.astype(BF)

    return call(
        kernel,
        (rows // tile,),
        [group_blocks(tile, width, g, per) for g in range(count)]
        + [pl.BlockSpec((width, cols), lambda i, c: (0, c[0]), pipeline_mode=pl.Buffered(1))]
        + [whole((1, TILE))] * 2 + [row_blocks(tile, TILE)] * 2,
        [row_blocks(tile, q_cols), row_blocks(tile, 2 * kv_cols), row_blocks(tile, raw_cols)],
        [shaped((rows, q_cols), BF), shaped((rows, 2 * kv_cols), BF), shaped((rows, raw_cols), F32)],
        "project_heads",
        scalars=[core],
    )(*groups, weight_all, q_gain, k_gain, cos, sin)


def head_grads(parts, raw, first_tile, heads, gain, cos, sin):
    rows, cols = parts[0].shape
    normed = (heads + 1) // 2
    count, tile = len(parts), 256

    def kernel(*refs):
        ds, (raw_ref, gain_ref, cos_ref, sin_ref, g_ref, sum_ref) = refs[:count], refs[count:]
        lane = lane_of((tile, TILE))
        even, first = lane < HEAD_SIZE, lane % HEAD_SIZE < HEAD_SIZE // 2
        cos, sin, gain = cos_ref[...], sin_ref[...], gain_ref[...]

        @pl.when(pl.program_id(0) == 0)
        def _():
            sum_ref[...] = jnp.zeros_like(sum_ref)

        for t in range(cols // TILE):
            at = slice(t * TILE, (t + 1) * TILE)
            d = sum(ref[:, at].astype(F32) for ref in ds)
            y = d
            if t < normed:
                x = raw_ref[:, at]
                r = lax.rsqrt(half_sums(x * x, even) * (1.0 / HEAD_SIZE) + EPS)
                n = x * r
                back = d * cos - turned(d, first) * sin
                dn = back * n
                w = back * gain
                y = r * (w - n * (half_sums(w * n, even) * (1.0 / HEAD_SIZE)))
                if heads - 2 * t == 1:
                    y = jnp.where(even, y, d)
                    dn = jnp.where(even, dn, 0.0)
                sum_ref[...] += jnp.sum(dn.reshape(tile // 8, 8, TILE), axis=0)
            g_ref[:, at] = y.astype(BF)

    raw_at = first_tile // normed
    return call(
        kernel,
        (rows // tile,),
        [row_blocks(tile, cols)] * count
        + [pl.BlockSpec((tile, normed * TILE), lambda i: (i, raw_at)), whole((1, TILE))]
        + [row_blocks(tile, TILE)] * 2,
        [row_blocks(tile, cols), whole((8, TILE))],
        [shaped((rows, cols), BF), shaped((8, TILE), F32)],
        "head_grads",
    )(*parts, raw, gain, cos, sin)


def stacked(ref, g, even):
    out = []
    for p in range(2):
        pair = ref[0, :, (2 * g + p) * TILE : (2 * g + p + 1) * TILE]
        zero = jnp.zeros_like(pair)
        out += [jnp.where(even, pair, zero), jnp.where(even, zero, pair)]
    return jnp.concatenate(out, axis=0)


def unstacked(values, p, even):
    base = 2 * p * TILE
    return jnp.where(even, values[base : base + TILE], values[base + TILE : base + 2 * TILE])


def transposed_pair(values, p, even):
    at = 2 * p * TILE
    low, high = values[:, at : at + TILE].T, values[:, at + TILE : at + 2 * TILE].T
    return jnp.where(even, low, high)


def widen(refs, heads, place):
    at = 0
    even = lane_of((TILE, TILE)) < HEAD_SIZE
    for ref in refs:
        for r in range(0, ref.shape[1], TILE):
            for t in range(heads):
                x = ref[0, r : r + TILE, t * TILE : (t + 1) * TILE].astype(F32)
                other = pltpu.roll(x, HEAD_SIZE, 1)
                for part, value in enumerate((jnp.where(even, x, other), jnp.where(even, other, x))):
                    n = 2 * t + part
                    col = slice((n % heads) * TILE, (n % heads + 1) * TILE)
                    place(n < heads, slice(at, at + TILE), col, value)
            at += TILE


def narrow(k_ref, v_ref, rows, t, heads, even):
    tiles = []
    for n in (2 * t, 2 * t + 1):
        ref = k_ref if n < heads else v_ref
        x = ref[rows, (n % heads) * TILE : (n % heads + 1) * TILE]
        tiles.append(x + pltpu.roll(x, HEAD_SIZE, 1))
    return jnp.where(even, tiles[0], tiles[1])


def key_bias(qseg_ref, kseg_ref, j, i, blocks):
    at = pl.ds(pl.multiple_of(j * TILE, TILE), TILE)
    key_at = lax.broadcasted_iota(jnp.int32, (TILE, TILE), 0) + j * TILE
    query_at = lane_of((TILE, TILE)) + (i + blocks) * TILE
    ok = (kseg_ref[0, at, :] == qseg_ref[0, pl.ds(i, 1), :]) & (key_at <= query_at)
    return at, jnp.concatenate([jnp.where(ok, 0.0, -1e30)] * 4, axis=1)


def attend(low_block, q, kv_prior, kv, qseg, kseg):
    batch, rows, cols = q.shape
    blocks = rows // TILE
    heads = kv.shape[2] // TILE
    keys = 2 * rows
    lse_rows = -(-4 * heads // 8) * 8

    def kernel(lo_ref, q_ref, prior_ref, kv_ref, qseg_ref, kseg_ref, o_ref, lse_ref, acc_ref, sum_ref, k_ref, v_ref):
        b, i = pl.program_id(0), pl.program_id(1)
        lane = lane_of((TILE, TILE))
        even = lane < HEAD_SIZE

        @pl.when(i == 0)
        def _():
            def place(is_key, at, col, value):
                (k_ref if is_key else v_ref)[at, col] = value.astype(BF)

            widen((prior_ref, kv_ref), heads, place)

        qs = [stacked(q_ref, g, even) * jnp.asarray(SCALE, BF) for g in range(heads)]
        acc_ref[...] = jnp.zeros_like(acc_ref)
        sum_ref[...] = jnp.zeros_like(sum_ref)
        seg = qseg_ref[0]
        row_at = lax.broadcasted_iota(jnp.int32, (TILE, TILE), 0) + (i + blocks) * TILE

        def step(j, carry):
            at = pl.ds(pl.multiple_of(j * TILE, TILE), TILE)
            ok = (seg == kseg_ref[0, pl.ds(j, 1), :]) & (lane + j * TILE <= row_at)
            bias = jnp.where(ok, 0.0, -1e30)
            bias = jnp.concatenate([bias] * 4, axis=0)
            for g in range(heads):
                col = slice(g * TILE, (g + 1) * TILE)
                e = jnp.exp(dot_nt(qs[g], k_ref[at, col]) + bias)
                sum_ref[g] += e
                acc_ref[g] += dot(e.astype(BF), v_ref[at, col])
            return carry

        lax.fori_loop(lo_ref[b * blocks + i], i + blocks + 1, step, 0)
        lse = jnp.zeros((TILE, TILE), F32)
        for g in range(heads):
            total = jnp.sum(sum_ref[g], axis=-1, keepdims=True)
            out = acc_ref[g] / total
            log = jnp.log(total)
            for p in range(2):
                o_ref[0, :, (2 * g + p) * TILE : (2 * g + p + 1) * TILE] = unstacked(out, p, even).astype(BF)
            for h in range(4):
                lse = jnp.where(lane == 4 * g + h, log[h * TILE : (h + 1) * TILE], lse)
        lse_ref[0, 0] = lse.T[:lse_rows]

    per_q = lambda n: pl.BlockSpec((1, TILE, n), lambda b, i, lo: (b, i, 0))
    per_b = lambda s: pl.BlockSpec((1,) + s[1:], lambda b, i, lo: (b, 0, 0))
    return call(
        kernel,
        (batch, blocks),
        [per_q(cols), per_b(kv.shape), per_b(kv.shape), per_q(1), per_b(kseg.shape)],
        [per_q(cols), pl.BlockSpec((1, 1, lse_rows, TILE), lambda b, i, lo: (b, i, 0, 0))],
        [shaped(q.shape, BF), shaped((batch, blocks, lse_rows, TILE), F32)],
        "attend",
        [pltpu.VMEM((heads, 4 * TILE, TILE), F32)] * 2 + [pltpu.VMEM((keys, heads * TILE), BF)] * 2,
        [low_block],
    )(q, kv_prior, kv, qseg, kseg)


def attend_back(low_block, q, kv_prior, kv, qseg, kseg, o, lse, do):
    batch, rows, cols = q.shape
    blocks = rows // TILE
    heads = kv.shape[2] // TILE
    keys = 2 * rows

    def kernel(lo_ref, q_ref, prior_ref, kv_ref, qseg_ref, kseg_ref, o_ref, lse_ref, do_ref, dq_ref, dprior_ref, dkv_ref, acc_ref, k_ref, kt_ref, v_ref, dk_ref, dv_ref):
        b, i = pl.program_id(0), pl.program_id(1)
        even = lane_of((TILE, TILE)) < HEAD_SIZE

        @pl.when(i == 0)
        def _():
            def place(is_key, at, col, value):
                if is_key:
                    k_ref[at, col] = value.astype(BF)
                    kt_ref[col, at] = value.T.astype(BF)
                else:
                    v_ref[at, col] = value.astype(BF)

            widen((prior_ref, kv_ref), heads, place)
            dk_ref[...] = jnp.zeros_like(dk_ref)
            dv_ref[...] = jnp.zeros_like(dv_ref)

        qs = [stacked(q_ref, g, even) * jnp.asarray(SCALE, BF) for g in range(heads)]
        dos = [stacked(do_ref, g, even) for g in range(heads)]
        lses, deltas = [], []
        for g in range(heads):
            each = []
            for p in range(2):
                at = slice((2 * g + p) * TILE, (2 * g + p + 1) * TILE)
                both = (o_ref[0, :, at].astype(F32) * do_ref[0, :, at].astype(F32)).T
                each += [
                    jnp.sum(both[n : n + HEAD_SIZE], axis=0, keepdims=True)
                    for n in (0, HEAD_SIZE)
                ]
            deltas.append(jnp.concatenate(each, axis=1))
            lses.append(
                jnp.concatenate([lse_ref[0, 0, 4 * g + h : 4 * g + h + 1, :] for h in range(4)], axis=1)
            )
        acc_ref[...] = jnp.zeros_like(acc_ref)

        def step(j, carry):
            at, bias = key_bias(qseg_ref, kseg_ref, j, i, blocks)
            for g in range(heads):
                col = slice(g * TILE, (g + 1) * TILE)
                p = jnp.exp(dot_nt(k_ref[at, col], qs[g]) + (bias - lses[g]))
                ds = (p * (dot_nt(v_ref[at, col], dos[g]) - deltas[g])).astype(BF)
                dv_ref[at, col] += dot(p.astype(BF), dos[g])
                dk_ref[at, col] += dot(ds, qs[g])
                acc_ref[g] += dot(kt_ref[col, at], ds)
            return carry

        lax.fori_loop(lo_ref[b * blocks + i], i + blocks + 1, step, 0)
        for g in range(heads):
            for p in range(2):
                dq_ref[0, :, (2 * g + p) * TILE : (2 * g + p + 1) * TILE] = (
                    transposed_pair(acc_ref[g], p, even) * SCALE
                )

        @pl.when(i == blocks - 1)
        def _():
            for r in range(0, rows, TILE):
                for t in range(heads):
                    col = slice(t * TILE, (t + 1) * TILE)
                    dprior_ref[0, r : r + TILE, col] = narrow(
                        dk_ref, dv_ref, slice(r, r + TILE), t, heads, even
                    ).astype(BF)
                    dkv_ref[0, r : r + TILE, col] = narrow(
                        dk_ref, dv_ref, slice(rows + r, rows + r + TILE), t, heads, even
                    )

    per_q = lambda n: pl.BlockSpec((1, TILE, n), lambda b, i, lo: (b, i, 0))
    per_b = lambda s: pl.BlockSpec((1,) + s[1:], lambda b, i, lo: (b, 0, 0))
    wide = (keys, heads * TILE)
    return call(
        kernel,
        (batch, blocks),
        [per_q(cols), per_b(kv.shape), per_b(kv.shape), per_b(qseg.shape), per_b(kseg.shape)]
        + [per_q(cols), pl.BlockSpec((1, 1) + lse.shape[2:], lambda b, i, lo: (b, i, 0, 0))]
        + [per_q(cols)],
        [per_q(cols), per_b(kv.shape), per_b(kv.shape)],
        [shaped(q.shape, F32), shaped(kv.shape, BF), shaped(kv.shape, F32)],
        "attend_back",
        [
            pltpu.VMEM((heads, TILE, 4 * TILE), F32),
            pltpu.VMEM(wide, BF),
            pltpu.VMEM(wide[::-1], BF),
            pltpu.VMEM(wide, BF),
            pltpu.VMEM(wide, F32),
            pltpu.VMEM(wide, F32),
        ],
        [low_block],
    )(q, kv_prior, kv, qseg, kseg, o, lse, do)


def hidden_units(hidden, low, gate_up, down):
    half, width = hidden[0].shape
    cols = down.shape[0]
    tile = 256
    per = half // tile
    count = len(hidden)

    def kernel(*refs):
        hid, lows = refs[:count], refs[count : 2 * count]
        gu_ref, wd_ref, act_ref, grad_ref = refs[2 * count :]
        x, y = pick_group(hid, per), pick_group(lows, per)
        step = 256
        for c in range(0, cols, step):
            n = min(step, cols - c)
            gate = dot(x, gu_ref[:, c : c + n])
            up = dot(x, gu_ref[:, cols + c : cols + c + n])
            grad = dot_nt(y, wd_ref[c : c + n, :])
            sig = 1.0 / (1.0 + jnp.exp(-gate))
            silu = gate * sig
            act_ref[:, c : c + n] = (silu * up).astype(BF)
            grad_ref[:, c : c + n] = (grad * up * (sig * (1.0 + gate * (1.0 - sig)))).astype(BF)
            grad_ref[:, cols + c : cols + c + n] = (grad * silu).astype(BF)

    groups = [group_blocks(tile, width, g, per) for g in range(count)]
    rows = count * half
    return call(
        kernel,
        (rows // tile,),
        groups + groups + [once(gate_up.shape), once(down.shape)],
        [row_blocks(tile, cols), row_blocks(tile, 2 * cols)],
        [shaped((rows, cols), BF), shaped((rows, 2 * cols), BF)],
        "hidden_units",
    )(*hidden, *low, gate_up, down)


def tall_grad(groups, rights, bit, name):
    half, width = groups[0].shape
    cols = rights[0].shape[1]
    count, pairs = len(groups), len(rights)
    tile = 512
    steps = width // tile
    split = bit is not None
    side = steps // 2 if split else 0

    def kernel(bit_ref, *refs):
        lefts, right, outs = refs[:count], refs[count : count + pairs], refs[count + pairs :]
        total = None
        for g in range(count):
            r = right[g // 2][(g % 2) * half : (g % 2 + 1) * half, :]
            term = dot_tn(lefts[g][...], r)
            total = term if total is None else total + term

        @pl.when(pl.program_id(0) >= side)
        def _():
            outs[0][...] = total.astype(BF)

        if split:

            @pl.when(pl.program_id(0) < side)
            def _():
                outs[1][...] = total.astype(BF)

    def column(i, bit):
        if not split:
            return (0, i)
        return (0, i % side + side * jnp.where(i >= side, bit[0], 1 - bit[0]))

    out_specs = [pl.BlockSpec((tile, cols), lambda i, b: (jnp.maximum(i - side, 0), 0))]
    if split:
        out_specs.append(pl.BlockSpec((tile, cols), lambda i, b: (jnp.minimum(i, side - 1), 0)))
    return call(
        kernel,
        (steps,),
        [pl.BlockSpec((half, tile), column)] * count + [once(r.shape) for r in rights],
        out_specs,
        [shaped(((steps - side) * tile, cols), BF)] * len(out_specs),
        name,
        scalars=[bit if split else 0],
    )(*groups, *rights)


def wide_grad(lefts, groups, name):
    half, width = groups[0].shape
    cols = lefts[0].shape[1]
    count, pairs = len(groups), len(lefts)
    tile = 512

    def kernel(*refs):
        total = None
        for g in range(count):
            left = refs[g // 2][(g % 2) * half : (g % 2 + 1) * half, :]
            term = dot_tn(left, refs[pairs + g][...])
            total = term if total is None else total + term
        refs[-1][...] = total.astype(BF)

    return call(
        kernel,
        (width // tile,),
        [once(a.shape) for a in lefts] + [pl.BlockSpec((half, tile), lambda i: (0, i))] * count,
        pl.BlockSpec((cols, tile), lambda i: (0, i)),
        shaped((cols, width), BF),
        name,
    )(*lefts, *groups)


def sum_products(lefts, rights, transposed, name, core=0, part=None):
    rows = lefts[0].shape[0]
    width = rights[0].shape[0] if transposed else rights[0].shape[1]
    tile, count = 512, len(lefts)

    def kernel(core_ref, *refs):
        total = None
        for a, b in zip(refs[:count], refs[count : 2 * count]):
            term = dot_nt(a[...], b[...]) if transposed else dot(a[...], b[...])
            total = term if total is None else total + term
        refs[-2][...] = total[: rows // 2]
        refs[-1][...] = total[rows // 2 :].astype(BF)

    at = lambda c: c[0] if part else 0
    if transposed:
        right = [
            pl.BlockSpec((tile, part or r.shape[1]), lambda i, c: (i, at(c))) for r in rights
        ]
    else:
        right = [
            pl.BlockSpec((part or r.shape[0], tile), lambda i, c: (at(c), i)) for r in rights
        ]
    column = pl.BlockSpec((rows // 2, tile), lambda i, c: (0, i))
    return call(
        kernel,
        (width // tile,),
        [once(a.shape) for a in lefts] + right,
        [column, column],
        [shaped((rows // 2, width), F32), shaped((rows // 2, width), BF)],
        name,
        scalars=[core],
    )(*lefts, *rights)


def first_sum(grad_q, grad_kv, weights, core):
    rows, part = grad_kv.shape
    width, tile = weights.shape[0], 512
    count = grad_q.shape[1] // part + 1

    def kernel(core_ref, *refs):
        total = None
        for a, b in zip(refs[:count], refs[count : 2 * count]):
            term = dot_nt(a[...], b[...])
            total = term if total is None else total + term
        refs[-2][...] = total[: rows // 2]
        refs[-1][...] = total[rows // 2 :].astype(BF)

    column_of = lambda n: pl.BlockSpec(
        (rows, part), lambda i, c: (0, n), pipeline_mode=pl.Buffered(1)
    )
    weight_of = lambda n: pl.BlockSpec((tile, part), lambda i, c: (i, count * c[0] + n))
    column = pl.BlockSpec((rows // 2, tile), lambda i, c: (0, i))
    return call(
        kernel,
        (width // tile,),
        [column_of(n) for n in range(count - 1)] + [column_of(0)]
        + [weight_of(n) for n in range(count)],
        [column, column],
        [shaped((rows // 2, width), F32), shaped((rows // 2, width), BF)],
        "first_sum",
        scalars=[core],
    )(*[grad_q] * (count - 1), grad_kv, *[weights] * count)


def token_product(groups, weight, core, part, name):
    half, width = groups[0].shape
    tile = 256
    per, count = half // tile, len(groups)

    def kernel(core_ref, *refs):
        refs[-1][...] = dot_nt(pick_group(refs[:count], per), refs[count][...]).astype(BF)

    return call(
        kernel,
        (count * per,),
        [group_blocks(tile, width, g, per) for g in range(count)]
        + [pl.BlockSpec((part, width), lambda i, c: (c[0], 0), pipeline_mode=pl.Buffered(1))],
        row_blocks(tile, part),
        shaped((count * half, part), BF),
        name,
        scalars=[core],
    )(*groups, weight)


def unit_moves(groups, size, pieces, padded):
    moves = []
    for n in range(2):
        for j, (a, b) in enumerate(pieces):
            for owner in range(4 * groups):
                at = ((2 * j + n) * groups + owner // 4) * padded
                moves.append((n, owner % 4, owner * size + a, at, b - a))
    return moves


def split_units(gate, up, groups, size, pieces, padded):
    rows, cols = gate.shape
    moves = unit_moves(groups, size, pieces, padded)
    share = 2 * len(pieces) * groups * padded

    def kernel(gate_ref, up_ref, out_ref, wide, kinds):
        kinds[...] = jnp.zeros_like(kinds)
        for n, ref in enumerate((gate_ref, up_ref)):
            wide[...] = ref[...].astype(F32)
            for m, c, src, dst, width in moves:
                if m == n:
                    kinds[c, :, dst : dst + width] = wide[:, src : src + width]
        out_ref[...] = kinds[...].astype(BF)

    out = shaped((4, rows, share), BF)
    return call(
        kernel,
        (1,),
        [whole((rows, cols))] * 2,
        whole(out.shape),
        out,
        "split_units",
        [pltpu.VMEM((rows, cols), F32), pltpu.VMEM(out.shape, F32)],
    )(gate, up)


def join_units(classes, groups, size, pieces, padded):
    rows = classes[0].shape[0]
    moves = unit_moves(groups, size, pieces, padded)

    def kernel(a_ref, b_ref, c_ref, d_ref, gate_ref, up_ref):
        for n, c, src, dst, width in moves:
            ref = (a_ref, b_ref, c_ref, d_ref)[c]
            (gate_ref, up_ref)[n][:, src : src + width] = ref[:, dst : dst + width]

    out = shaped((rows, 4 * groups * size), F32)
    return call(
        kernel,
        (1,),
        [whole(classes[0].shape)] * 4,
        [whole(out.shape)] * 2,
        [out] * 2,
        "join_units",
    )(*classes)


QUERY_HEADS = 24
KEY_VALUE_HEADS = 6
AXES = ("seq", "z", "x", "core")
CHUNKS = 2
UNITS, DOWN, OUT, QKV = range(4)
PLAN = {
    (UNITS, 0): (0, 2, 3),
    (DOWN, 0): (0, 2, 3),
    (UNITS, 1): (3, 5, 6),
    (DOWN, 1): (3, 5, 6),
    (DOWN, 0, True): (7, 9, 11),
    (UNITS, 0, True): (7, 9, 11),
    (DOWN, 1, True): (9, 14, 15),
    (UNITS, 1, True): (11, 12, 13),
    (OUT, 0, True): (14, 15, 16, 17),
    (OUT, 1, True): (12, 13, 15, 16),
    (QKV, 0, True): (13, 14, 15, 16),
    (QKV, 1, True): (14, 15, 16, 17),
}


def swap_core(value):
    return lax.ppermute(value, "core", [(0, 1), (1, 0)])


def core_pick(first, second):
    return jnp.where(lax.axis_index("core") == 0, first, second)


def core_concat(own, other, axis=0):
    return core_pick(
        jnp.concatenate([own, other], axis=axis), jnp.concatenate([other, own], axis=axis)
    )


def swap_seq(value):
    return lax.ppermute(value, "seq", [(0, 1), (1, 0)])


def swap_x(value):
    return lax.ppermute(value, "x", [(0, 1), (1, 0)])


def x_pick(first, second):
    return jnp.where(lax.axis_index("x") == 0, first, second)


def group_axes():
    bits = lax.axis_size("z").bit_length() - 1
    return [("seq", 1)] + [("z", 1 << k) for k in reversed(range(bits))]


def orders_of(name):
    cube = group_axes()
    far, near, seq = cube[1:-1], cube[-1:], cube[:1]
    what, number = name[:2]
    if what in (OUT, QKV):
        x = [("x", 1)]
        cube = cube + x
        stages = [far, seq, near, x] if number else [far, x, near, seq]
    else:
        stages = [far, seq, near] if what == DOWN else [far, near, seq]
    return cube, [s[::-1] for s in stages[::-1]] if len(name) > 2 else stages


def hop_bit(hop):
    axis, step = hop
    return lax.axis_index(axis) // step % 2


def exchange(value, hop):
    axis, step = hop
    return lax.ppermute(value, axis, [(i, i ^ step) for i in range(lax.axis_size(axis))])


def place_kernel(bit_ref, own_ref, got_ref, out_ref):
    bit = bit_ref[0]
    out_ref[:, pl.ds(bit, 1)] = own_ref[...][:, None]
    out_ref[:, pl.ds(1 - bit, 1)] = got_ref[...][:, None]


def placed(own, got, dim, bit):
    shape = own.shape
    lead, inner = math.prod(shape[:dim]), math.prod(shape[dim:-2])
    flat = (lead, inner) + shape[-2:]
    part = math.gcd(inner, 2) if lead == 1 else inner
    block = (1, part) + shape[-2:]
    side = pl.BlockSpec(block, lambda i, j, bit: (i, j, 0, 0))
    out = call(
        place_kernel,
        (lead, inner // part),
        [side, side],
        pl.BlockSpec((1, 2) + block[1:], lambda i, j, bit: (i, 0, j, 0, 0)),
        shaped((lead, 2) + flat[1:], own.dtype),
        "place",
        scalars=[bit],
    )(own.reshape(flat), got.reshape(flat))
    return out.reshape(shape[:dim] + (2,) + shape[dim + 1 :])


class Values:
    def __init__(self):
        for name in ("low", "hidden", "wgu", "wd", "act", "ggu", "keep", "home", "hidden_sum", "down_sum"):
            setattr(self, name, {})


class Flow:
    def __init__(self):
        self.live = Values()
        self.rest, self.flight, self.later, self.stage, self.now = {}, {}, {}, {}, 0

    def fence(self):
        values, parts = lax.optimization_barrier((vars(self.live), self.rest))
        vars(self.live).update(values)
        self.rest = parts

    def gather(self, name, block):
        self.rest[name] = block.reshape((1,) * len(orders_of(name)[0]) + block.shape)
        self.stage[name] = 0

    def scatter(self, name, rows, grad, sent=None):
        self.stage[name] = 0
        shape = [2] * len(orders_of(name)[0])
        if sent is None:
            self.rest[name] = grad.reshape(shape + [rows, grad.shape[1]])
        else:
            shape[self.hop(name)[1]] = 1
            self.rest[name] = tuple(v.reshape(shape + [rows, v.shape[1]]) for v in (grad, sent))

    def hop(self, name):
        cube, stages = orders_of(name)
        hop = sum(stages, [])[self.stage[name]]
        return hop, cube.index(hop)

    def start(self, name):
        hop, dim = self.hop(name)
        bit, value = hop_bit(hop), self.rest.pop(name)
        if isinstance(value, tuple):
            value, sent = value
        elif len(name) > 2:
            sent = lax.dynamic_slice_in_dim(value, 1 - bit, 1, dim)
        else:
            sent = value
        self.flight[name] = (value, exchange(sent, hop), dim, bit)

    def land(self, name):
        keep, got, dim, bit = self.flight.pop(name)
        self.stage[name] += 1
        stages = orders_of(name)[1]
        ends = [sum(map(len, stages[: k + 1])) for k in range(len(stages))]
        last = self.stage[name] == ends[-1]
        if len(name) > 2:
            if keep.shape[dim] == 2:
                keep = lax.dynamic_slice_in_dim(keep, bit, 1, dim)
            total = keep.astype(F32) + got.astype(F32)
            self.rest[name] = total if last else total.astype(BF)
        elif last:
            self.rest[name] = (keep, got)
            self.stage[name] = (dim, bit)
        else:
            self.rest[name] = placed(keep, got, dim, bit)
        if not last and self.stage[name] not in ends:
            self.start(name)
            self.land(name)

    def take(self, name):
        value = self.rest.pop(name)
        dims = len(orders_of(name)[0])
        if len(name) > 2:
            return value.reshape(value.shape[dims:])
        value = placed(*value, *self.stage[name])
        return value.reshape((-1,) + value.shape[dims + 1 :])

    def post(self, value, name, key=None, wait=0):
        self.later[name, key] = (value, self.now + wait)

    def interval(self, *work):
        active = [name for name, at in PLAN.items() if self.now in at]
        for name in active:
            self.start(name)
        for piece in work:
            piece()
        for name in active:
            self.land(name)
        for name, key in [n for n, (_, at) in self.later.items() if at == self.now]:
            value = self.later.pop((name, key))[0]
            if key is None:
                setattr(self.live, name, value)
            else:
                getattr(self.live, name)[key] = value
        self.fence()
        self.now += 1


def row_norm(values):
    scale = lax.rsqrt(jnp.mean(values * values, axis=-1, keepdims=True) + EPS)
    return values * scale, scale


def norm_back(grad, normed, scale, gain):
    u = grad * gain
    return scale * (u - normed * jnp.mean(u * normed, axis=-1, keepdims=True))


def doc_positions(segment_row):
    length = segment_row.shape[-1]
    places = jnp.arange(length, dtype=jnp.int32)
    earlier = jnp.concatenate([segment_row[..., :1] + 1, segment_row[..., :-1]], axis=-1)
    starts = jnp.where(segment_row != earlier, places, 0)
    latest = jnp.max(
        jnp.where(places[None, :] <= places[:, None], starts[..., None, :], 0), axis=-1
    )
    return places - latest


def rotary_tables(positions):
    pair_count = HEAD_SIZE // 2
    frequencies = jnp.exp(
        jnp.arange(pair_count, dtype=F32) * (-2.0 * math.log(10000.0) / HEAD_SIZE)
    )
    phases = positions.astype(F32)[..., None] * frequencies
    cos, sin = jnp.cos(phases), jnp.sin(phases)
    return jnp.tile(cos, (1, 4)), jnp.tile(jnp.concatenate([-sin, sin], axis=1), (1, 2))


def split_rows(rows, pieces):
    units, rest = rows // 8, rows % 8
    sizes = [8 * (units // pieces + (i < units % pieces)) for i in range(pieces)]
    sizes[-1] += rest
    ends = [sum(sizes[: i + 1]) for i in range(pieces)]
    return [(e - s, e) for s, e in zip(sizes, ends)]


def halves(w):
    n = w.shape[1] // 2
    return w[:, :n], w[:, n:]


def body(
    tokens,
    segments,
    attn_gain,
    w_query,
    key_projection_weight,
    value_projection_weight,
    query_norm_gain,
    key_gain,
    w_out,
    ffn_gain,
    w_gate,
    w_up,
    w_down,
    cotangent,
):
    _, half, width = tokens.shape
    ny, nz, nx = (lax.axis_size(a) for a in ("seq", "z", "x"))
    groups = ny * nz
    core, seq, x_at = (lax.axis_index(a) for a in ("core", "seq", "x"))
    q_cols, kv_cols = w_query.shape[1] // 2, key_projection_weight.shape[1] // 2
    kv_heads = KEY_VALUE_HEADS // 2
    out_rows, ff_rows, in_rows = w_out.shape[0], w_down.shape[0], w_gate.shape[0]
    pieces = split_rows(ff_rows, CHUNKS)
    step = TILE // math.gcd(TILE, groups)
    padded = -(-max(b - a for a, b in pieces) // step) * step
    share = groups * padded
    flow = Flow()
    do = lambda f, *a: (lambda: f(*a))

    def pair(value):
        return [value, swap_core(value)]

    def trade(value):
        return lax.ppermute(value, ("seq", "core"), [(0, 0), (1, 2), (2, 1), (3, 3)])

    weights = (w_query, key_projection_weight, value_projection_weight)
    lows, highs = zip(*(halves(w) for w in weights))
    gains = jnp.pad(jnp.stack([attn_gain, ffn_gain], axis=1), ((0, 0), (0, TILE - 2)))
    block = jnp.concatenate(lows + highs + (gains,), axis=1)
    block = jnp.concatenate(
        [block, jnp.pad(w_out, ((0, 0), (0, block.shape[1] - width)))], axis=0
    )
    gathered = lax.all_gather(block, AXES, axis=0)

    quarters = split_units(w_gate, w_up, groups, ff_rows, pieces, padded)
    mine = [core_pick(quarters[2 * x], quarters[2 * x + 1]) for x in range(2)]
    theirs = [core_pick(quarters[2 * x + 1], quarters[2 * x]) for x in range(2)]
    sent = x_pick(jnp.concatenate(theirs), jnp.concatenate(theirs[::-1]))
    got = swap_core(sent)
    near = core_concat(x_pick(mine[0], mine[1]), got[:in_rows])
    far = swap_x(core_concat(x_pick(mine[1], mine[0]), got[in_rows:]))
    block = x_pick(jnp.concatenate([near, far]), jnp.concatenate([far, near]))
    live = flow.live
    for j, (a, b) in enumerate(pieces):
        units_block = block[:, 2 * j * share : 2 * (j + 1) * share]
        down_block = jnp.pad(w_down[a:b], ((0, padded - b + a), (0, 0)))
        flow.gather((UNITS, j), units_block)
        flow.gather((DOWN, j), down_block)

    def take_gathered():
        live = flow.live
        live.gathered = gathered
        live.qkv = gathered[:, :in_rows].reshape(width, -1)

    def take_out():
        live = flow.live
        live.out = live.gathered[:, in_rows:, :width].reshape(-1, width)
        del live.gathered

    def tables():
        live = flow.live
        segments_pair = jnp.concatenate(pair(segments), axis=0)
        positions = doc_positions(segments_pair)
        own_start = seq * half
        own_positions = lax.dynamic_slice_in_dim(positions, own_start, half, 1)
        order_ids = jnp.where(segments_pair < 0, 1 << 20, segments_pair)
        own_ids = lax.dynamic_slice_in_dim(order_ids, own_start, half, 1)
        prior_ids = lax.dynamic_slice_in_dim(order_ids, jnp.maximum(own_start - half, 0), half, 1)
        prior_ids = jnp.where(own_start >= half, prior_ids, -2)
        key_ids = jnp.concatenate([prior_ids, own_ids], axis=1)
        low_block = jnp.sum(key_ids[:, None, :] < own_ids[:, ::TILE, None], axis=-1) // TILE
        live.low_block = low_block.astype(jnp.int32)
        live.query_rows, live.query_columns = own_ids.reshape(2, -1, TILE), own_ids[:, :, None]
        live.key_rows, live.key_columns = key_ids.reshape(2, -1, TILE), key_ids[:, :, None]
        live.cos, live.sin = rotary_tables(own_positions.reshape(2 * half))
        live.q_gain = jnp.tile(query_norm_gain.astype(F32), 2).reshape(1, TILE)
        live.k_gain = jnp.tile(key_gain.astype(F32), 2).reshape(1, TILE)

    def first_norm():
        live = flow.live
        live.low[0] = pair(cotangent.reshape(half, width))
        live.normed, live.scale = row_norm(tokens.reshape(half, width).astype(F32))

    def far_low():
        flow.post(swap_x(flow.live.low[0][0]), "far_low")

    def near_low():
        flow.live.low[1] = pair(flow.live.far_low)

    def first_hidden():
        live = flow.live
        n = q_cols + 2 * kv_cols
        live.gains = live.qkv[:, 2 * n : 2 * n + 2].T.astype(F32)
        live.hidden_first = pair((live.normed * live.gains[0]).astype(BF))

    def heads():
        live = flow.live
        q_rot, kv, live.raw = project(
            live.hidden_first, live.qkv, core, live.q_gain, live.k_gain, live.cos,
            live.sin, q_cols, kv_cols,
        )
        live.q, live.kv = q_rot.reshape(2, half, -1), kv.reshape(2, half, -1)

    def prior_keys():
        flow.post(swap_seq(flow.live.kv), "prior_kv")

    def attention():
        live = flow.live
        attn, live.lse = attend(
            live.low_block, live.q, live.prior_kv, live.kv, live.query_columns, live.key_rows
        )
        live.attn = attn.reshape(2 * half, q_cols)

    def near_rows(sums):
        return sums[0] + swap_core(sums[1]).astype(F32)

    def branch_sum():
        live = flow.live
        live.branch = sum_products([live.attn], [live.out], False, "branch", core, q_cols)

    def branch():
        live = flow.live
        live.middle = tokens.reshape(half, width).astype(F32) + near_rows(live.branch)
        live.normed2, live.scale2 = row_norm(live.middle)
        live.hidden[0] = pair((live.normed2 * live.gains[1]).astype(BF))

    def far_hidden():
        flow.post(swap_x(flow.live.hidden[0][0]), "far_hidden")

    def near_hidden():
        flow.live.hidden[1] = pair(flow.live.far_hidden)

    def units(j, h):
        live = flow.live
        if h == 0:
            live.wgu[j], live.wd[j] = flow.take((UNITS, j)), flow.take((DOWN, j))
        live.act[j, h], live.ggu[j, h] = hidden_units(
            live.hidden[h], live.low[h], live.wgu[j], live.wd[j]
        )

    def down_grad(j):
        live = flow.live
        acts = [live.act[j, h] for h in range(2)]
        grad = wide_grad(acts, live.low[0] + live.low[1], "down_grad")
        flow.scatter((DOWN, j, True), padded, grad)

    def units_grad(j):
        live = flow.live
        grads = [live.ggu[j, h] for h in range(2)]
        grads = tall_grad(live.hidden[0] + live.hidden[1], grads, seq, "units_grad")
        flow.scatter((UNITS, j, True), 4 * in_rows, *grads)

    def hidden_sum(h):
        live = flow.live
        js = range(CHUNKS)
        live.hidden_sum[h] = sum_products(
            [live.ggu[j, h] for j in js], [live.wgu[j] for j in js], True, "hidden_sum"
        )

    def far_hidden_sum():
        live = flow.live
        live.far_grad_sum = near_rows(live.hidden_sum.pop(1)).astype(BF)

    def near_hidden_sum():
        live = flow.live
        live.near_grad = near_rows(live.hidden_sum.pop(0))

    def far_grad():
        flow.post(swap_x(flow.live.far_grad_sum), "far_grad")

    def down_sum(h):
        live = flow.live
        js = range(CHUNKS)
        live.down_sum[h] = sum_products(
            [live.act[j, h] for j in js], [live.wd[j] for j in js], False, "down_sum"
        )

    def near_down_sums():
        live = flow.live
        live.far_result_sum = near_rows(live.down_sum.pop(1)).astype(BF)
        live.near_result = near_rows(live.down_sum.pop(0))

    def far_result():
        flow.post(swap_x(flow.live.far_result_sum), "far_result")

    def second_back():
        live = flow.live
        grad = live.near_grad + live.far_grad.astype(F32)
        live.grad_middle = cotangent.reshape(half, width).astype(F32) + norm_back(
            grad, live.normed2, live.scale2, live.gains[1]
        )
        live.grad_branch = pair(live.grad_middle.astype(BF))

    def out_grad():
        live = flow.live
        live.grad_attn = token_product(
            live.grad_branch, live.out, core, q_cols, "grad_attn"
        )
        grad = wide_grad([live.attn], live.grad_branch, "out_grad")
        grad = grad.reshape(nz * nx, 2, out_rows, width).transpose(1, 0, 2, 3)
        grad = grad.reshape(groups * nx * out_rows, width)
        flow.scatter((OUT, 0, True), out_rows, grad[:, : width // 2])
        flow.scatter((OUT, 1, True), out_rows, grad[:, width // 2 :])

    def attention_back():
        live = flow.live
        dq, live.sent_dkv, live.dkv = attend_back(
            live.low_block, live.q, live.prior_kv, live.kv, live.query_rows,
            live.key_columns, live.attn.reshape(2, half, q_cols), live.lse,
            live.grad_attn.reshape(2, half, q_cols),
        )
        live.dq = dq.reshape(2 * half, q_cols)

    def prior_back():
        flow.post(swap_seq(flow.live.sent_dkv), "prior_dkv")

    def queries_back():
        live = flow.live
        live.grad_q, live.q_part = head_grads(
            [live.dq], live.raw, 0, q_cols // HEAD_SIZE, live.q_gain, live.cos, live.sin
        )
        grads = tall_grad(live.hidden_first, [live.grad_q], seq, "q_grad")
        flow.scatter((QKV, 0, True), 2 * in_rows, *grads)

    def keys_back():
        live = flow.live
        tall = lambda v: v.reshape(2 * half, -1)
        live.grad_kv, k_part = head_grads(
            [tall(live.dkv), tall(live.prior_dkv)], live.raw, q_cols // TILE,
            kv_cols // HEAD_SIZE, live.k_gain, live.cos, live.sin,
        )
        grad = tall_grad(live.hidden_first, [live.grad_kv], None, "kv_grad")
        flow.scatter((QKV, 1, True), 2 * in_rows, grad[0])
        parts = jnp.stack([live.q_part, k_part]).sum(axis=1)
        live.head_gains = parts.reshape(2, 2, HEAD_SIZE).sum(axis=1)

    def first_sums():
        live = flow.live
        live.first = first_sum(live.grad_q, live.grad_kv, live.qkv, core)

    def first_back():
        live = flow.live
        live.input_grad = live.grad_middle + norm_back(
            near_rows(live.first), live.normed, live.scale, live.gains[0]
        )

    def finish_output():
        live = flow.live
        total = live.near_result + live.far_result.astype(F32)
        live.output = (live.middle + total).astype(BF)

    def gain_hops(hops):
        for hop in hops:
            flow.live.head_gains = flow.live.head_gains + exchange(flow.live.head_gains, hop)

    def home(j):
        rows = flow.take((UNITS, j, True)).reshape(2, 2 * in_rows, -1)
        flow.live.keep[j] = x_pick(rows[0], rows[1])
        flow.post(swap_x(x_pick(rows[1], rows[0])), "home", j)

    def own_shard(block):
        block = block.reshape(2, in_rows, -1)
        got = swap_core(core_pick(block[1], block[0]))
        return core_pick(block[0], block[1]), got

    def gain_grad(gain, pairs):
        total = sum(jnp.sum(w.astype(F32) * g, axis=1) for w, g in pairs)
        return total / gain.astype(F32)

    def finish_units():
        live = flow.live
        classes = []
        near, far = (
            own_shard(jnp.concatenate([v[j] for j in range(CHUNKS)], axis=1))
            for v in (live.keep, live.home)
        )
        for x in range(2):
            keep, got = (x_pick(*((n, f) if x == 0 else (f, n))) for n, f in zip(near, far))
            classes += [core_pick(keep, got), core_pick(got, keep)]
        live.grad_wg, live.grad_wu = join_units(classes, groups, ff_rows, pieces, padded)
        live.ffn_gain = gain_grad(ffn_gain, ((w_gate, live.grad_wg), (w_up, live.grad_wu)))
        downs = [flow.take((DOWN, j, True))[: b - a] for j, (a, b) in enumerate(pieces)]
        live.grad_wd = jnp.concatenate(downs, axis=0)

    def finish_out():
        grad = jnp.concatenate([flow.take((OUT, n, True)) for n in range(2)], axis=1)
        flow.live.grad_wo = trade(grad)

    gain_order = [("core", 1), ("x", 1)] + group_axes()
    schedule = (
        (tables, first_norm, take_gathered),
        (first_hidden,),
        (heads, prior_keys, take_out),
        (far_low, attention, branch_sum),
        (branch, near_low),
        (far_hidden, do(units, 0, 0)),
        (near_hidden, do(units, 0, 1), do(down_grad, 0), do(units_grad, 0)),
        (do(units, 1, 0), do(units, 1, 1), do(down_grad, 1), do(hidden_sum, 1)),
        (far_hidden_sum,),
        (far_grad, do(units_grad, 1), do(hidden_sum, 0), do(down_sum, 1), do(down_sum, 0)),
        (near_hidden_sum, second_back, near_down_sums),
        (far_result, out_grad, attention_back),
        (prior_back, do(home, 0), queries_back),
        (keys_back,),
        (first_sums, do(home, 1)),
        (first_back, finish_output, do(gain_hops, gain_order[:2])),
        (do(gain_hops, gain_order[2:4]),),
        (finish_units, do(gain_hops, gain_order[4:])),
    )
    for work in schedule:
        flow.interval(*work)
    finish_out()
    live = flow.live

    grads = []
    for n in range(2):
        keep, got = own_shard(flow.take((QKV, n, True)))
        grads.append((core_pick(keep, got), core_pick(got, keep)))
    grad_wq = jnp.concatenate(grads[0], axis=1)
    grad_wk = jnp.concatenate([g[:, :kv_cols] for g in grads[1]], axis=1)
    grad_wv = jnp.concatenate([g[:, kv_cols:] for g in grads[1]], axis=1)
    attn_gain_grad = gain_grad(attn_gain, zip(weights, (grad_wq, grad_wk, grad_wv)))
    return (
        live.output.reshape(1, half, width),
        live.input_grad.reshape(1, half, width),
        attn_gain_grad,
        grad_wq,
        grad_wk,
        grad_wv,
        live.head_gains[0],
        live.head_gains[1],
        live.grad_wo,
        live.ffn_gain,
        live.grad_wg,
        live.grad_wu,
        live.grad_wd,
    )


def solution(mesh):
    ny, nf = mesh.shape["seq"], mesh.shape["fsdp"]
    fine = Mesh(mesh.devices.reshape(ny, nf // 4, 2, 2), AXES)
    fsdp = ("z", "x", "core")
    rows = P(fsdp, "seq", None)
    vec, mat = P(AXES), P(AXES, None)
    in_specs = (rows, P(fsdp, None), vec, mat, mat, mat, P(), P(), mat, vec, mat, mat, mat, rows)
    out_specs = (rows, rows, vec, mat, mat, mat, P(), P(), mat, vec, mat, mat, mat)
    return jax.shard_map(body, mesh=fine, in_specs=in_specs, out_specs=out_specs, check_vma=False)
```
